32 devices in a mesh: dp: 16 (over z, y, x), section: 2 (over core).
Axes of the slice: x: 2, y: 2, z: 4, core: 2. Of those that a mesh axis runs over, the one named last changes fastest.
Arguments:
- path_table: bfloat16 [512, 2048], replicated, may hold values from -6 to 6
- tokens: int32 [16, 8, 48], P('dp'), may hold values from 0 to 511
- assign: int32 [16, 8], P('dp'), may hold values from 0 to 7, each once within a row
- out_grad: bfloat16 [16, 2, 4, 48, 2048], P('dp'), may hold values from -6 to 6
- query_weights: bfloat16 [2, 2048, 128], P('section', 'dp'), may hold values from -1 to 24
- gain: bfloat16 [2, 2048], P('section', 'dp'), may hold values from 0.5 to 1.5
- scale: bfloat16 [2, 2048], P('section', 'dp'), may hold values from 0.14 to 1.82
Outputs:
- query_grad: float32 [2, 2048, 128], P('section', 'dp')
- gain_grad: float32 [2, 2048], P('section', 'dp')
- scale_grad: float32 [2, 2048], P('section', 'dp')
The draws below stay inside these ranges and needn't reach their ends.
All inputs are finite; a program needn't handle non-finite values.
Results may differ from the reference program's by a relative error of at most 0.0031.
Values may be sent and summed in bfloat16 or wider, within the bound.
A program may use at most 64 MiB of HBM per device.

```python
import math
import jax
import jax.numpy as jnp
import numpy as np
from jax import lax

D = 2048
HD = 128
VOCAB = 512
SEQ = 48
MICRO = 4
BLOCKS = 2
N_DP = 16


def shared_offset(key):
    offset_key = jax.random.fold_in(key, 7001)
    magnitude = jax.random.uniform(jax.random.fold_in(offset_key, 1), (D,), jnp.float32, 0.3, 0.6)
    flipped = jax.random.bernoulli(jax.random.fold_in(offset_key, 2), 0.5, (D,))
    return magnitude * jnp.where(flipped, 1.0, -1.0)


def draw_path_table(key, part):
    own_key = jax.random.fold_in(key, 11)
    values = jax.random.truncated_normal(own_key, -5.0, 5.0, (VOCAB, D), jnp.float32)
    return (values + shared_offset(key)[None, :]).astype(jnp.bfloat16)


def draw_out_grad(key, part):
    own_key = jax.random.fold_in(key, 13)
    shape_full = (N_DP, 2, MICRO, SEQ, D)
    values = jax.random.truncated_normal(own_key, -5.0, 5.0, shape_full, jnp.float32)
    return (values + shared_offset(key)[None, None, None, None, :]).astype(jnp.bfloat16)


def draw_query_weights(key, part):
    base = jax.random.truncated_normal(key, -3.0, 3.0, (BLOCKS, D, HD), jnp.float32) * HD ** (-0.5)
    return base.astype(jnp.bfloat16)


def draw_scale(key, part):
    level = jnp.arange(BLOCKS, dtype=jnp.float32) / (BLOCKS - 1)
    rising = 0.3 * jnp.power(3.0, level)
    jitter = jnp.exp(jax.random.uniform(key, (BLOCKS, D), jnp.float32, -0.69, 0.69))
    return (rising[:, None] * jitter).astype(jnp.bfloat16)


def plant(array, rng, least, high):
    dims = array.shape
    index_at = [jax.random.randint(jax.random.fold_in(rng, axis), (), 0, dims[axis]) for axis in range(len(dims))]
    array = array.at[tuple(index_at)].set(least)
    longest = dims.index(max(dims))
    index_at[longest] = (index_at[longest] + 1) % dims[longest]
    return array.at[tuple(index_at)].set(high)


def rank_table(amount, lean):
    portions = [(1 << 20) // math.isqrt(grade ** lean) + 1 for grade in range(1, amount + 1)]
    spread = 1 + sum(portions) // (1 << 30)
    return np.cumsum(np.array([max(1, weight // spread) for weight in portions]))


def ranked_ids(key, shape, number_of, slope):
    table = rank_table(number_of, slope)
    lot = jax.random.randint(jax.random.fold_in(key, 1), shape, 0, int(table[number_of - 1]))
    grade = jnp.searchsorted(jnp.asarray(table, jnp.int32), lot, side="right")
    return jax.random.permutation(jax.random.fold_in(key, 2), number_of)[grade].astype(jnp.int32)


def setup_inputs(seed: int = 0) -> dict:
    arg_keys = jax.random.split(jax.random.key(seed), 8)
    return {
        "path_table": draw_path_table(jax.random.fold_in(arg_keys[7], 71), 0),
        "tokens": plant(ranked_ids(arg_keys[1], (N_DP, 2 * MICRO, SEQ), VOCAB, 2), jax.random.fold_in(arg_keys[1], 3), 0, VOCAB - 1).astype(jnp.int32),
        "assign": jax.vmap(lambda own: jax.random.permutation(own, 2 * MICRO))(jax.random.split(arg_keys[2], N_DP)).reshape((N_DP, 2 * MICRO)).astype(jnp.int32),
        "out_grad": draw_out_grad(jax.random.fold_in(arg_keys[7], 71), 0),
        "query_weights": draw_query_weights(jax.random.fold_in(arg_keys[7], 71), 0),
        "gain": jnp.clip(1.0 + 0.1 * jax.random.normal(arg_keys[5], (BLOCKS, D), jnp.float32), 0.5, 1.5).astype(jnp.bfloat16),
        "scale": draw_scale(jax.random.fold_in(arg_keys[7], 71), 0),
    }


HIGH = lax.Precision.HIGHEST

def block_apply(stream_in, query_map, gain_vec, scale_vec):
    batch_count, seq_len, model_width = stream_in.shape
    head_size = query_map.shape[1]
    head_count = model_width // head_size
    stream = stream_in.astype(jnp.float32)
    mean_square = lax.optimization_barrier(jnp.mean(stream * stream, axis=-1, keepdims=True))
    normed = stream * lax.rsqrt(mean_square + 1e-05) * gain_vec
    normed = lax.optimization_barrier(normed.astype(jnp.bfloat16)).astype(jnp.float32)
    heads_in = normed.reshape(batch_count, seq_len, head_count, head_size)
    query_heads = query_map.reshape(head_count, head_size, head_size)
    queries = jnp.einsum('nshi,hij->nshj', heads_in, query_heads, precision=HIGH) * (1.0 / math.sqrt(head_size))
    queries = lax.optimization_barrier(queries.astype(jnp.bfloat16)).astype(jnp.float32)
    scores = jnp.einsum('nshj,nthj->nhst', queries, heads_in, precision=HIGH)
    causal = lax.broadcasted_iota(jnp.int32, (seq_len, seq_len), 0) >= lax.broadcasted_iota(jnp.int32, (seq_len, seq_len), 1)
    scores = jnp.where(causal, scores, -1e+30)
    row_max = lax.optimization_barrier(jnp.max(scores, axis=-1, keepdims=True))
    raised = jnp.exp(scores - row_max)
    attend = raised / lax.optimization_barrier(jnp.sum(raised, axis=-1, keepdims=True))
    attend = lax.optimization_barrier(attend.astype(jnp.bfloat16)).astype(jnp.float32)
    mixed = jnp.einsum('nhst,nthj->nshj', attend, heads_in, precision=HIGH).reshape(batch_count, seq_len, model_width)
    return (stream + scale_vec * mixed).astype(jnp.bfloat16)

def reference(path_table, tokens, assign, out_grad, query_weights, gain, scale):
    slot_tokens = jnp.take_along_axis(tokens, assign[:, :, None].astype(jnp.int32), axis=1)
    start_stream = jnp.take(path_table, slot_tokens.reshape(-1, SEQ), axis=0)
    params = (query_weights.astype(jnp.float32), gain.astype(jnp.float32), scale.astype(jnp.float32))

    def model(layer_params):
        stream = start_stream
        for block_index in range(BLOCKS):
            stream = block_apply(stream, layer_params[0][block_index], layer_params[1][block_index], layer_params[2][block_index])
        return stream
    final_stream, pullback = jax.vjp(model, params)
    (query_raw, gain_raw, scale_raw), = pullback(out_grad.reshape(final_stream.shape))
    total = jnp.sum(query_raw * query_raw) + jnp.sum(gain_raw * gain_raw) + jnp.sum(scale_raw * scale_raw)
    factor = jnp.minimum(1.0, math.sqrt(float(BLOCKS * D * (HD + 2))) / jnp.sqrt(total))
    return (query_raw * factor, gain_raw * factor, scale_raw * factor)
```

```python
import functools
import math

import jax
import jax.numpy as jnp
from jax import lax
from jax.experimental import pallas as pl
from jax.experimental.pallas import tpu as pltpu
from jax.sharding import PartitionSpec as P

MESH = pl.DeviceIdType.MESH
F32 = jnp.float32
BF16 = jnp.bfloat16
TAIL = 16
PLANE = 4
BLOCKS = 2
UNROLL = 32


def matmul(lhs, rhs, lhs_dim, rhs_dim):
    return lax.dot_general(
        lhs, rhs, (((lhs_dim,), (rhs_dim,)), ((), ())), preferred_element_type=F32
    )


def beside(parts, axis):
    return parts[0] if len(parts) == 1 else jnp.concatenate(parts, axis=axis)


def diagonal(parts):
    zero = jnp.zeros_like(parts[0])
    return beside(
        [
            beside([part if i == k else zero for k in range(len(parts))], 1)
            for i, part in enumerate(parts)
        ],
        0,
    )


def layout(n_dp, n_sec, width, hd):
    plane = math.gcd(n_dp, min(PLANE, width // hd // n_sec))
    return plane, n_dp // plane, width // hd // n_sec // plane


def step_kernel(
    n_dp,
    n_sec,
    table,
    tokens,
    assign,
    out_grad,
    weights,
    gain,
    scale,
    out,
    tokens_in,
    assign_in,
    gain_in,
    scale_in,
    packed,
    params,
    toks,
    tbl,
    emb,
    cot,
    xs,
    normed,
    queries,
    mixed,
    probs,
    dnormed,
    rstd,
    roots,
    parts,
    grads,
    tails,
    tx,
    rx,
    norms,
    in_sem,
    load_sem,
    emb_sem,
    t_send,
    t_recv,
    w_send,
    w_recv,
    c_send,
    c_recv,
    x_send,
    x_recv,
    g_send,
    g_recv,
    n_send,
    n_recv,
):
    slots, seq = tokens.shape
    vocab, width = table.shape
    rows, hd = weights.shape
    plane, planes, heads = layout(n_dp, n_sec, width, hd)
    layers = n_sec
    per_head = hd // rows
    n_dev = n_dp * n_sec
    members = plane * n_sec
    held = heads * hd
    some = slots // BLOCKS * seq
    block_rows = plane * some
    two = 2 * seq
    pairs = block_rows // two
    inv = 1.0 / math.sqrt(hd)
    me_d = lax.axis_index("dp")
    me_s = lax.axis_index("section")
    me = me_d * n_sec + me_s
    me_z = lax.div(me_d, plane)
    me_p = lax.rem(me_d, plane)
    member = me_p * n_sec + me_s

    def repeat(first, last, body):
        if last - first <= UNROLL:
            for k in range(first, last):
                body(k)
        else:

            def step(k, carry):
                body(k)
                return carry

            lax.fori_loop(first, last, step, 0)

    def head_of(p, c, hh):
        return (c * heads + hh) * plane + p

    def columns(h):
        return pl.ds(pl.multiple_of(h * hd, hd), hd)

    def lanes(hh):
        return slice(hh * hd, (hh + 1) * hd)

    def remote(src, dst, ssem, rsem, d, s):
        return pltpu.make_async_remote_copy(
            src_ref=src,
            dst_ref=dst,
            send_sem=ssem,
            recv_sem=rsem,
            device_id=(d, s),
            device_id_type=MESH,
        )

    barrier = pltpu.get_barrier_semaphore()

    def greet(k):
        t = lax.rem(me + k, n_dev)
        pl.semaphore_signal(
            barrier,
            inc=1,
            device_id=(lax.div(t, n_sec), lax.rem(t, n_sec)),
            device_id_type=MESH,
        )

    pltpu.make_async_copy(table, tbl, load_sem).start()
    loads = [
        pltpu.make_async_copy(tokens, tokens_in, in_sem.at[0]),
        pltpu.make_async_copy(assign, assign_in, in_sem.at[1]),
        pltpu.make_async_copy(weights, packed.at[pl.ds(0, rows)], in_sem.at[2]),
        pltpu.make_async_copy(gain, gain_in, in_sem.at[3]),
        pltpu.make_async_copy(scale, scale_in, in_sem.at[4]),
    ]
    for load in loads:
        load.start()
    repeat(1, n_dev, greet)
    own_columns = [
        pltpu.make_async_copy(
            table.at[:, columns(head_of(me_p, me_s, hh))], emb.at[:, lanes(hh)], emb_sem.at[hh]
        )
        for hh in range(heads)
    ]
    for load in own_columns:
        load.start()

    def cot_at(blk, p, hh):
        return cot.at[blk, hh, pl.ds(p * some, some)]

    def cot_from(blk, h):
        return out_grad.at[pl.ds(blk * some, some), columns(h)]

    for blk in range(BLOCKS):
        for hh in range(heads):
            pltpu.make_async_copy(
                cot_from(blk, head_of(me_p, me_s, hh)), cot_at(blk, me_p, hh), c_recv.at[blk]
            ).start()

    for load in loads:
        load.wait()
    tail_row = lax.broadcasted_iota(jnp.int32, (TAIL, hd), 0)
    packed[rows : rows + TAIL, :] = jnp.where(
        tail_row == 0,
        gain_in[...].astype(F32),
        jnp.where(tail_row == 1, scale_in[...].astype(F32), 0.0),
    ).astype(BF16)
    toks[me_p] = beside(
        [tokens_in[pl.ds(assign_in[j], 1), :].astype(F32) for j in range(slots)], 1
    )
    probs[...] = jnp.zeros(probs.shape, F32)

    pltpu.make_async_copy(tbl, tbl, load_sem).wait()
    chunk = math.gcd(vocab, 128)
    lane_chunk = lax.broadcasted_iota(jnp.int32, (chunk, hd), 1)

    def table_norm(i, carry):
        at = pl.ds(pl.multiple_of(i * chunk, chunk), chunk)
        squares = jnp.zeros((chunk, hd), F32)
        for h in range(width // hd):
            block = tbl[at, h * hd : (h + 1) * hd].astype(F32)
            squares = squares + block * block
        root = lax.rsqrt(jnp.sum(squares, axis=1, keepdims=True) * (1.0 / width) + 1e-05)
        high = root.astype(BF16).astype(F32)
        mid = (root - high).astype(BF16).astype(F32)
        low = root - high - mid
        emb[at, held : held + hd] = jnp.where(
            lane_chunk == 0,
            high,
            jnp.where(lane_chunk == 1, mid, jnp.where(lane_chunk == 2, low, 0.0)),
        ).astype(BF16)
        return carry

    lax.fori_loop(0, vocab // chunk, table_norm, 0)

    pl.semaphore_wait(barrier, n_dev - 1)

    for k in range(1, plane):
        p = lax.rem(me_p + k, plane)
        remote(toks.at[me_p], toks.at[me_p], t_send, t_recv, me_z * plane + p, me_s).start()

    my_head = lax.div(me_d * rows, hd)
    to_p = lax.rem(my_head, plane)
    to_i = lax.div(my_head, plane)
    to_s = lax.div(to_i, heads)
    place = lax.rem(to_i, heads) * per_head + lax.rem(me_d, per_head)
    keep = (to_p == me_p) & (to_s == me_s)

    def give(k):
        z = lax.rem(me_z + k, planes)
        remote(
            packed, params.at[me_s, place], w_send, w_recv.at[me_s], z * plane + to_p, to_s
        ).start()

    repeat(1, planes, give)

    @pl.when(keep)
    def _():
        pltpu.make_async_copy(packed, params.at[me_s, place], w_recv.at[me_s]).start()

    @pl.when(jnp.logical_not(keep))
    def _():
        remote(
            packed,
            params.at[me_s, place],
            w_send,
            w_recv.at[me_s],
            me_z * plane + to_p,
            to_s,
        ).start()

    def send_cot(blk):
        for k in range(1, plane):
            p = lax.rem(me_p + k, plane)
            for hh in range(heads):
                remote(
                    cot_from(blk, head_of(p, me_s, hh)),
                    cot_at(blk, me_p, hh),
                    c_send,
                    c_recv.at[blk],
                    me_z * plane + p,
                    me_s,
                ).start()

    send_cot(0)

    ones_row = jnp.ones((TAIL, 2 * hd), BF16)
    ones_column = jnp.ones((TAIL, hd), BF16)

    def as_row(terms):
        high = terms.astype(BF16)
        low = (terms - high.astype(F32)).astype(BF16)
        return matmul(ones_row, beside([high, low], 1), 1, 1)[0:1]

    def as_column(row):
        at = lax.broadcasted_iota(jnp.int32, (TAIL, row.shape[1]), 0)
        high = row.astype(BF16).astype(F32)
        mid = (row - high).astype(BF16).astype(F32)
        low = row - high - mid
        stack = jnp.where(at == 0, high, jnp.where(at == 1, mid, jnp.where(at == 2, low, 0.0)))
        return matmul(stack.astype(BF16), ones_column, 0, 0)

    def exchange(phase, blk, terms):
        parts[phase, blk, member] = as_row(terms)

        def share(k):
            t = lax.rem(member + k, members)
            remote(
                parts.at[phase, blk, member],
                parts.at[phase, blk, member],
                x_send,
                x_recv.at[phase, blk],
                me_z * plane + lax.div(t, n_sec),
                lax.rem(t, n_sec),
            ).start()

        repeat(1, members, share)

    def exchanged(phase, blk):
        if members > 1:
            whole = parts.at[phase, blk, pl.ds(0, members - 1)]
            pltpu.make_async_copy(whole, whole, x_recv.at[phase, blk]).wait()
        return jnp.sum(parts[phase, blk], axis=0)

    def layer_param(b, hh):
        at = hh * per_head
        tail = params[b, at, rows:, :].astype(F32)
        weight = params[b, at, :rows, :]
        if per_head > 1:
            for i in range(1, per_head):
                tail = tail + params[b, at + i, rows:, :].astype(F32)
            weight = jnp.concatenate(
                [params[b, at + i, :rows, :] for i in range(per_head)], axis=0
            )
        return weight, tail[0:1], tail[1:2]

    def layer_params(b):
        found = [layer_param(b, hh) for hh in range(heads)]
        return (
            diagonal([one[0] for one in found]),
            beside([one[1] for one in found], 1),
            beside([one[2] for one in found], 1),
        )

    at_row = lax.broadcasted_iota(jnp.int32, (seq, two), 0)
    at_col = lax.broadcasted_iota(jnp.int32, (seq, two), 1)
    first = at_col < seq
    allowed = at_row <= jnp.where(first, at_col, at_col - seq)
    wide_col = lax.broadcasted_iota(jnp.int32, (seq, hd), 1)
    wide_first = wide_col < seq
    wide_second = (wide_col >= seq) & (wide_col < two)
    vocab_lane = lax.broadcasted_iota(jnp.int32, (some, hd), 1).astype(F32)

    def wide(column):
        return beside([column] * heads, 1)

    def both(sides):
        return sides[:, :hd] if heads == 1 else sum(sides[:, lanes(hh)] for hh in range(heads))

    def embed(blk):
        for p in range(plane):
            col = as_column(toks[p, :, blk * some : (blk + 1) * some])
            picked = beside(
                [
                    jnp.where(vocab_lane + float(v * hd) == col, 1.0, 0.0).astype(BF16)
                    for v in range(vocab // hd)
                ],
                1,
            )
            found = matmul(picked, emb[...], 1, 0)
            at = slice(p * some, (p + 1) * some)
            xs[0, blk, at] = found[:, :held].astype(BF16)
            root = jnp.sum(found[:, held:], axis=1, keepdims=True)
            rstd[0, blk, at] = jnp.broadcast_to(root, (some, hd))

    def forward(b, blk):
        if b > 0:
            root = lax.rsqrt(exchanged(b - 1, blk) * (1.0 / width) + 1e-05)
            roots[b, blk] = root
            rstd[b, blk] = as_column(root)
        weight, gain_row, scale_row = layer_params(b)
        norm = (xs[b, blk].astype(F32) * wide(rstd[b, blk]) * gain_row).astype(BF16)
        normed[b, blk] = norm
        query = (matmul(norm, weight, 1, 0) * inv).astype(BF16)
        queries[b, blk] = query
        tiles = [(p, hh) for p in range(pairs) for hh in range(heads)]
        scores = []
        for p, hh in tiles:
            lo, mid, hi = p * two, p * two + seq, (p + 1) * two
            scores.append(
                matmul(
                    beside([norm[lo:mid, lanes(hh)], norm[mid:hi, lanes(hh)]], 1),
                    diagonal([query[lo:mid, lanes(hh)], query[mid:hi, lanes(hh)]]),
                    1,
                    1,
                )
            )
        spread = {}
        for (p, hh), score in zip(tiles, scores):
            score = jnp.where(allowed, score, -1e30)
            raised = jnp.exp(score - jnp.max(score, axis=0, keepdims=True))
            attend = raised * (1.0 / jnp.sum(raised, axis=0, keepdims=True))
            probs[b, blk, p, hh, :, 0:two] = attend
            attend = attend.astype(BF16)
            zero = jnp.zeros_like(attend)
            spread[p, hh] = [jnp.where(first, attend, zero), jnp.where(first, zero, attend)]
        terms = []
        for p in range(pairs):
            lo, hi = p * two, (p + 1) * two
            mix = matmul(
                beside([part for hh in range(heads) for part in spread[p, hh]], 0),
                diagonal([norm[lo:hi, lanes(hh)] for hh in range(heads)]),
                0,
                0,
            )
            mixed[b, blk, lo:hi] = mix
            if b + 1 < layers:
                out_rows = (xs[b, blk, lo:hi].astype(F32) + scale_row * mix).astype(BF16)
                xs[b + 1, blk, lo:hi] = out_rows
                out_rows = out_rows.astype(F32)
                terms.append(both(out_rows * out_rows))
        if b + 1 < layers:
            exchange(b, blk, beside(terms, 0))

    def backward(b, blk):
        if b + 1 == layers:
            pltpu.make_async_copy(cot.at[blk], cot.at[blk], c_recv.at[blk]).wait()
        else:
            inner = exchanged(layers - 1 + b, blk) * (1.0 / width)
            root = roots[b + 1, blk]
            along = as_column(inner * root * root * root)
            _, gain_row, _ = layer_params(b + 1)
            dy = dnormed[blk].astype(F32) * gain_row
            for hh in range(heads):
                back = rstd[b + 1, blk] * dy[:, lanes(hh)]
                back = back - xs[b + 1, blk, :, lanes(hh)].astype(F32) * along
                cot[blk, hh] = (cot[blk, hh].astype(F32) + back).astype(BF16)
        weight, gain_row, scale_row = layer_params(b)
        given = beside([cot[blk, hh] for hh in range(heads)], 1).astype(F32)
        scale_part = jnp.sum(given * mixed[b, blk], axis=0, keepdims=True)
        dmix = (given * scale_row).astype(BF16)
        tiles = [(p, hh) for p in range(pairs) for hh in range(heads)]
        gap = jnp.zeros((hd - two, hd), BF16)
        wide_gap = jnp.zeros((hd - two, 2 * hd), BF16)
        datts = []
        for p, hh in tiles:
            lo, mid, hi = p * two, p * two + seq, (p + 1) * two
            datts.append(
                matmul(
                    beside(
                        [normed[b, blk, lo:mid, lanes(hh)], normed[b, blk, mid:hi, lanes(hh)]], 1
                    ),
                    beside(
                        [diagonal([dmix[lo:mid, lanes(hh)], dmix[mid:hi, lanes(hh)]]), wide_gap],
                        0,
                    ),
                    1,
                    1,
                )
            )
        dscores, attends = {}, {}
        for (p, hh), datt in zip(tiles, datts):
            datt = datt.astype(BF16).astype(F32)
            attend = probs[b, blk, p, hh]
            inner = jnp.sum(datt * attend, axis=0, keepdims=True)
            dscore = (attend * (datt - inner)).astype(BF16)
            attend = attend.astype(BF16)
            zero = jnp.zeros_like(dscore)
            dscores[p, hh] = beside(
                [jnp.where(wide_first, dscore, zero), jnp.where(wide_second, dscore, zero)], 0
            )
            attends[p, hh] = beside(
                [jnp.where(wide_first, attend, zero), jnp.where(wide_second, attend, zero)], 0
            )
        dqueries, dnorms = [], []
        for p in range(pairs):
            lo, hi = p * two, (p + 1) * two
            dquery = matmul(
                beside([dscores[p, hh] for hh in range(heads)], 0),
                diagonal([normed[b, blk, lo:hi, lanes(hh)] for hh in range(heads)]),
                0,
                0,
            )
            dqueries.append(dquery[:two].astype(BF16))
            dnorms.append(
                beside(
                    [
                        matmul(
                            beside([dscores[p, hh], attends[p, hh]], 1),
                            beside(
                                [
                                    queries[b, blk, lo:hi, lanes(hh)],
                                    gap,
                                    dmix[lo:hi, lanes(hh)],
                                    gap,
                                ],
                                0,
                            ),
                            1,
                            0,
                        )
                        for hh in range(heads)
                    ],
                    1,
                )
            )
        dquery = beside(dqueries, 0)
        dnorm = beside(dnorms, 0) + matmul(dquery, weight, 1, 1) * inv
        for hh in range(heads):
            grad = matmul(normed[b, blk, :, lanes(hh)], dquery[:, lanes(hh)], 0, 0)
            if blk > 0:
                grad = grad + grads[hh]
            grads[hh] = grad
        dnorm = dnorm.astype(BF16)
        if b > 0:
            dnormed[blk] = dnorm
        dnorm = dnorm.astype(F32)
        x_in = xs[b, blk].astype(F32)
        gain_part = jnp.sum(dnorm * (x_in * wide(rstd[b, blk])), axis=0, keepdims=True)
        if blk > 0:
            gain_part = gain_part + tails[0:1]
            scale_part = scale_part + tails[1:2]
        tails[0:1] = gain_part
        tails[1:2] = scale_part
        if b > 0:
            exchange(layers - 2 + b, blk, both(dnorm * gain_row * x_in))

    def send_grads(b):
        for hh in range(heads):
            gain_part, scale_part = tails[0:1, lanes(hh)], tails[1:2, lanes(hh)]
            gain_hi = gain_part.astype(BF16).astype(F32)
            scale_hi = scale_part.astype(BF16).astype(F32)
            tail = jnp.where(
                tail_row == 0,
                gain_hi,
                jnp.where(
                    tail_row == 1,
                    gain_part - gain_hi,
                    jnp.where(
                        tail_row == 2,
                        scale_hi,
                        jnp.where(tail_row == 3, scale_part - scale_hi, 0.0),
                    ),
                ),
            ).astype(BF16)
            dweight = (grads[hh] * inv).astype(BF16)
            for i in range(per_head):
                at = hh * per_head + i
                tx[b, at, 0:rows] = dweight[i * rows : (i + 1) * rows]
                tx[b, at, rows : rows + TAIL] = tail
        for hh in range(heads):
            for i in range(per_head):
                at = hh * per_head + i
                r = head_of(me_p, me_s, hh) * per_head + i
                mine = (r == me_d) & (me_s == b)

                @pl.when(mine)
                def _():
                    pltpu.make_async_copy(tx.at[b, at], rx.at[me_z], g_recv).start()

                @pl.when(jnp.logical_not(mine))
                def _():
                    remote(tx.at[b, at], rx.at[me_z], g_send, g_recv, r, b).start()

    for load in own_columns:
        load.wait()
    if plane > 1:
        pltpu.make_async_copy(
            toks.at[pl.ds(0, plane - 1)], toks.at[pl.ds(0, plane - 1)], t_recv
        ).wait()
    embed(0)
    for b in range(layers):
        pltpu.make_async_copy(params.at[b], params.at[b], w_recv.at[b]).wait()
        for blk in range(BLOCKS):
            if b == 0 and blk > 0:
                embed(blk)
            forward(b, blk)
            if b == 0 and blk + 1 < BLOCKS:
                send_cot(blk + 1)
            if b + 1 == layers:
                backward(b, blk)
    send_grads(layers - 1)
    for b in reversed(range(layers - 1)):
        for blk in range(BLOCKS):
            backward(b, blk)
        send_grads(b)

    pltpu.make_async_copy(rx, rx, g_recv).wait()
    total = jnp.sum(rx[...].astype(F32), axis=0)
    total_query = total[0:rows]
    total_gain = total[rows : rows + 1] + total[rows + 1 : rows + 2]
    total_scale = total[rows + 2 : rows + 3] + total[rows + 3 : rows + 4]
    if per_head > 1:
        at = lax.broadcasted_iota(jnp.int32, (1, hd), 1)
        start = lax.rem(me_d, per_head) * rows
        inside = (at >= start) & (at < start + rows)
        total_gain = jnp.where(inside, total_gain, 0.0)
        total_scale = jnp.where(inside, total_scale, 0.0)
    squares = (
        jnp.sum(total_query * total_query, axis=0, keepdims=True)
        + total_gain * total_gain
        + total_scale * total_scale
    )
    norms[pl.ds(me, 1)] = squares[None]

    def tell(k):
        t = lax.rem(me + k, n_dev)
        remote(
            norms.at[me], norms.at[me], n_send, n_recv, lax.div(t, n_sec), lax.rem(t, n_sec)
        ).start()

    repeat(1, n_dev, tell)

    if members > 1:
        for phase in range(2 * layers - 2):
            whole = parts.at[phase, :, pl.ds(0, members - 1)]
            pltpu.make_async_copy(whole, whole, x_send).wait()
    if plane > 1:
        sent = toks.at[pl.ds(0, plane - 1)]
        pltpu.make_async_copy(sent, sent, t_send).wait()
        sent = cot.at[:, :, pl.ds(0, (plane - 1) * some)]
        pltpu.make_async_copy(sent, sent, c_send).wait()

    def sent_weight(k, carry):
        pltpu.make_async_copy(packed, packed, w_send).wait()
        return carry

    lax.fori_loop(0, jnp.where(keep, planes - 1, planes), sent_weight, 0)

    def sent_grad(k, carry):
        pltpu.make_async_copy(packed, packed, g_send).wait()
        return carry

    pieces = layers * heads * per_head
    lax.fori_loop(0, jnp.where(keep, pieces - 1, pieces), sent_grad, 0)

    others = norms.at[pl.ds(0, n_dev - 1)]
    pltpu.make_async_copy(others, others, n_recv).wait()
    overall = jnp.sum(jnp.sum(norms[...], axis=0), axis=1, keepdims=True)
    limit = float(layers * width * (hd + 2))
    factor = jnp.minimum(1.0, math.sqrt(limit) / jnp.sqrt(overall))
    out[0:rows] = total_query * factor
    out[rows : rows + 8] = jnp.where(
        lax.broadcasted_iota(jnp.int32, (8, hd), 0) == 0, total_gain * factor, total_scale * factor
    )
    pltpu.make_async_copy(others, others, n_send).wait()


def split_kernel(found, query_grad, gain_grad, scale_grad):
    rows = query_grad.shape[0]
    query_grad[...] = found[0:rows]
    gain_grad[...] = found[rows : rows + 1]
    scale_grad[...] = found[rows + 1 : rows + 2]


def on_device(path_table, tokens, assign, out_grad, query_weights, gain, scale):
    n_dp = lax.axis_size("dp")
    n_sec = lax.axis_size("section")
    vocab, width = path_table.shape
    slots, seq = tokens.shape[1:]
    rows, hd = query_weights.shape[1:]
    count = slots * seq
    layers = n_sec
    plane, planes, heads = layout(n_dp, n_sec, width, hd)
    per_head = hd // rows
    pieces = heads * per_head
    n_dev = n_dp * n_sec
    held = heads * hd
    block_rows = plane * count // BLOCKS
    pairs = block_rows // (2 * seq)
    phases = max(1, 2 * layers - 2)
    first = lax.rem(lax.axis_index("dp") * rows, hd)
    if rows < hd:
        gain = lax.dynamic_update_slice(jnp.zeros((1, hd), BF16), gain, (0, first))
        scale = lax.dynamic_update_slice(jnp.zeros((1, hd), BF16), scale, (0, first))
    vmem = pl.BlockSpec(memory_space=pltpu.VMEM)
    hbm = pl.BlockSpec(memory_space=pl.ANY)
    stream = pltpu.VMEM((layers, BLOCKS, block_rows, held), BF16)
    found = pl.pallas_call(
        functools.partial(step_kernel, n_dp, n_sec),
        out_shape=pltpu.VMEM((rows + 8, hd), F32),
        in_specs=[hbm] * 7,
        out_specs=vmem,
        scratch_shapes=[
            pltpu.VMEM((slots, seq), jnp.int32),
            pltpu.SMEM((slots,), jnp.int32),
            pltpu.VMEM((1, hd), BF16),
            pltpu.VMEM((1, hd), BF16),
            pltpu.VMEM((rows + TAIL, hd), BF16),
            pltpu.VMEM((layers, pieces, rows + TAIL, hd), BF16),
            pltpu.VMEM((plane, 1, count), F32),
            pltpu.VMEM((vocab, width), BF16),
            pltpu.VMEM((vocab, held + hd), BF16),
            pltpu.VMEM((BLOCKS, heads, block_rows, hd), BF16),
            stream,
            stream,
            stream,
            pltpu.VMEM((layers, BLOCKS, block_rows, held), F32),
            pltpu.VMEM((layers, BLOCKS, pairs, heads, seq, hd), F32),
            pltpu.VMEM((BLOCKS, block_rows, held), BF16),
            pltpu.VMEM((layers, BLOCKS, block_rows, hd), F32),
            pltpu.VMEM((layers, BLOCKS, 1, block_rows), F32),
            pltpu.VMEM((phases, BLOCKS, plane * n_sec, 1, block_rows), F32),
            pltpu.VMEM((heads, hd, hd), F32),
            pltpu.VMEM((8, held), F32),
            pltpu.VMEM((layers, pieces, rows + TAIL, hd), BF16),
            pltpu.VMEM((planes, rows + TAIL, hd), BF16),
            pltpu.VMEM((n_dev, 1, hd), F32),
            pltpu.SemaphoreType.DMA((5,)),
            pltpu.SemaphoreType.DMA,
            pltpu.SemaphoreType.DMA((heads,)),
            pltpu.SemaphoreType.DMA,
            pltpu.SemaphoreType.DMA,
            pltpu.SemaphoreType.DMA,
            pltpu.SemaphoreType.DMA((layers,)),
            pltpu.SemaphoreType.DMA,
            pltpu.SemaphoreType.DMA((BLOCKS,)),
            pltpu.SemaphoreType.DMA,
            pltpu.SemaphoreType.DMA((phases, BLOCKS)),
            pltpu.SemaphoreType.DMA,
            pltpu.SemaphoreType.DMA,
            pltpu.SemaphoreType.DMA,
            pltpu.SemaphoreType.DMA,
        ],
        compiler_params=pltpu.CompilerParams(
            collective_id=0, has_side_effects=True, vmem_limit_bytes=56 * 1024 * 1024
        ),
    )(
        path_table,
        tokens[0],
        assign[0],
        out_grad.reshape(count, width),
        query_weights[0],
        gain,
        scale,
    )
    query_grad, gain_grad, scale_grad = pl.pallas_call(
        split_kernel,
        out_shape=(
            jax.ShapeDtypeStruct((rows, hd), F32),
            jax.ShapeDtypeStruct((1, hd), F32),
            jax.ShapeDtypeStruct((1, hd), F32),
        ),
        in_specs=[vmem],
        out_specs=(vmem, vmem, vmem),
        compiler_params=pltpu.CompilerParams(vmem_limit_bytes=1024 * 1024),
    )(found)
    if rows < hd:
        gain_grad = lax.dynamic_slice(gain_grad, (0, first), (1, rows))
        scale_grad = lax.dynamic_slice(scale_grad, (0, first), (1, rows))
    return query_grad[None], gain_grad, scale_grad


def solution(mesh):
    in_specs = (
        P(),
        P("dp", None, None),
        P("dp", None),
        P("dp", None, None, None, None),
        P("section", "dp", None),
        P("section", "dp"),
        P("section", "dp"),
    )
    out_specs = (P("section", "dp", None), P("section", "dp"), P("section", "dp"))
    return jax.shard_map(
        on_device, mesh=mesh, in_specs=in_specs, out_specs=out_specs, check_vma=False
    )
```

```python
import functools
import math

import jax
import jax.numpy as jnp
from jax import lax
from jax.experimental import pallas as pl
from jax.experimental.pallas import tpu as pltpu
from jax.sharding import PartitionSpec as P

MESH = pl.DeviceIdType.MESH
F32 = jnp.float32
BF16 = jnp.bfloat16
TAIL = 16
PLANE = 4
BLOCKS = 2
UNROLL = 32


def matmul(lhs, rhs, lhs_dim, rhs_dim):
    return lax.dot_general(
        lhs, rhs, (((lhs_dim,), (rhs_dim,)), ((), ())), preferred_element_type=F32
    )


def beside(parts, axis):
    return parts[0] if len(parts) == 1 else jnp.concatenate(parts, axis=axis)


def diagonal(parts):
    zero = jnp.zeros_like(parts[0])
    return beside(
        [
            beside([part if i == k else zero for k in range(len(parts))], 1)
            for i, part in enumerate(parts)
        ],
        0,
    )


def layout(n_dp, n_sec, width, hd):
    plane = math.gcd(n_dp, min(PLANE, width // hd // n_sec))
    return plane, n_dp // plane, width // hd // n_sec // plane


def step_kernel(
    n_dp,
    n_sec,
    table,
    tokens,
    assign,
    out_grad,
    weights,
    gain,
    scale,
    out,
    tokens_in,
    assign_in,
    gain_in,
    scale_in,
    packed,
    params,
    toks,
    tbl,
    emb,
    cot,
    xs,
    normed,
    queries,
    mixed,
    probs,
    dnormed,
    dqueried,
    rstd,
    roots,
    parts,
    grads,
    tails,
    tx,
    rx,
    tail_tx,
    tail_rx,
    norms,
    in_sem,
    load_sem,
    emb_sem,
    t_send,
    t_recv,
    w_send,
    w_recv,
    c_send,
    c_recv,
    x_send,
    x_recv,
    g_send,
    g_recv,
    tg_send,
    tg_recv,
    n_send,
    n_recv,
):
    slots, seq = tokens.shape
    vocab, width = table.shape
    rows, hd = weights.shape
    plane, planes, heads = layout(n_dp, n_sec, width, hd)
    layers = n_sec
    per_head = hd // rows
    n_dev = n_dp * n_sec
    members = plane * n_sec
    held = heads * hd
    some = slots // BLOCKS * seq
    block_rows = plane * some
    two = 2 * seq
    pairs = block_rows // two
    inv = 1.0 / math.sqrt(hd)
    me_d = lax.axis_index("dp")
    me_s = lax.axis_index("section")
    me = me_d * n_sec + me_s
    me_z = lax.div(me_d, plane)
    me_p = lax.rem(me_d, plane)
    member = me_p * n_sec + me_s

    def repeat(first, last, body):
        if last - first <= UNROLL:
            for k in range(first, last):
                body(k)
        else:

            def step(k, carry):
                body(k)
                return carry

            lax.fori_loop(first, last, step, 0)

    def after(at, k, size):
        moved = at + k
        return jnp.where(moved >= size, moved - size, moved)

    def peers(size, at, body):
        if size * n_sec <= UNROLL:
            for kd in range(size):
                d = after(at, kd, size) if kd else at
                for ks in range(n_sec):
                    if kd or ks:
                        body(d, after(me_s, ks, n_sec) if ks else me_s)
        else:

            def step(k, carry):
                t = lax.rem(at * n_sec + me_s + k, size * n_sec)
                body(lax.div(t, n_sec), lax.rem(t, n_sec))
                return carry

            lax.fori_loop(1, size * n_sec, step, 0)

    def head_of(p, c, hh):
        return (c * heads + hh) * plane + p

    def columns(h):
        return pl.ds(pl.multiple_of(h * hd, hd), hd)

    def lanes(hh):
        return slice(hh * hd, (hh + 1) * hd)

    def remote(src, dst, ssem, rsem, d, s):
        return pltpu.make_async_remote_copy(
            src_ref=src,
            dst_ref=dst,
            send_sem=ssem,
            recv_sem=rsem,
            device_id=(d, s),
            device_id_type=MESH,
        )

    barrier = pltpu.get_barrier_semaphore()

    def greet(d, s):
        pl.semaphore_signal(barrier, inc=1, device_id=(d, s), device_id_type=MESH)

    pltpu.make_async_copy(table, tbl, load_sem).start()
    loads = [
        pltpu.make_async_copy(tokens, tokens_in, in_sem.at[0]),
        pltpu.make_async_copy(assign, assign_in, in_sem.at[1]),
        pltpu.make_async_copy(weights, packed.at[pl.ds(0, rows)], in_sem.at[2]),
        pltpu.make_async_copy(gain, gain_in, in_sem.at[3]),
        pltpu.make_async_copy(scale, scale_in, in_sem.at[4]),
    ]
    for load in loads:
        load.start()
    peers(n_dp, me_d, greet)
    own_columns = [
        pltpu.make_async_copy(
            table.at[:, columns(head_of(me_p, me_s, hh))], emb.at[:, lanes(hh)], emb_sem.at[hh]
        )
        for hh in range(heads)
    ]
    for load in own_columns:
        load.start()

    def cot_at(blk, p, hh):
        return cot.at[blk, hh, pl.ds(p * some, some)]

    def cot_from(blk, h):
        return out_grad.at[pl.ds(blk * some, some), columns(h)]

    for blk in range(BLOCKS):
        for hh in range(heads):
            pltpu.make_async_copy(
                cot_from(blk, head_of(me_p, me_s, hh)), cot_at(blk, me_p, hh), c_recv.at[blk]
            ).start()

    for load in loads:
        load.wait()
    tail_row = lax.broadcasted_iota(jnp.int32, (TAIL, hd), 0)
    packed[rows : rows + TAIL, :] = jnp.where(
        tail_row == 0,
        gain_in[...].astype(F32),
        jnp.where(tail_row == 1, scale_in[...].astype(F32), 0.0),
    ).astype(BF16)
    toks[me_p] = beside(
        [tokens_in[pl.ds(assign_in[j], 1), :].astype(F32) for j in range(slots)], 1
    )
    probs[...] = jnp.zeros(probs.shape, F32)

    pl.semaphore_wait(barrier, n_dev - 1)

    my_head = lax.div(me_d * rows, hd)
    to_p = lax.rem(my_head, plane)
    to_i = lax.div(my_head, plane)
    to_s = lax.div(to_i, heads)
    place = lax.rem(to_i, heads) * per_head + lax.rem(me_d, per_head)
    keep = (to_p == me_p) & (to_s == me_s)

    def give(k):
        z = lax.rem(me_z + k, planes)
        remote(
            packed, params.at[me_s, place], w_send, w_recv.at[me_s], z * plane + to_p, to_s
        ).start()

    repeat(1, planes, give)
    for k in range(1, plane):
        p = lax.rem(me_p + k, plane)
        remote(toks.at[me_p], toks.at[me_p], t_send, t_recv, me_z * plane + p, me_s).start()

    @pl.when(keep)
    def _():
        pltpu.make_async_copy(packed, params.at[me_s, place], w_recv.at[me_s]).start()

    @pl.when(jnp.logical_not(keep))
    def _():
        remote(
            packed,
            params.at[me_s, place],
            w_send,
            w_recv.at[me_s],
            me_z * plane + to_p,
            to_s,
        ).start()

    def send_cot(blk):
        for k in range(1, plane):
            p = lax.rem(me_p + k, plane)
            for hh in range(heads):
                remote(
                    cot_from(blk, head_of(p, me_s, hh)),
                    cot_at(blk, me_p, hh),
                    c_send,
                    c_recv.at[blk],
                    me_z * plane + p,
                    me_s,
                ).start()

    send_cot(0)

    ones_row = jnp.ones((TAIL, 2 * hd), BF16)
    ones_column = jnp.ones((TAIL, hd), BF16)

    def as_row(terms):
        high = terms.astype(BF16)
        low = (terms - high.astype(F32)).astype(BF16)
        return matmul(ones_row, beside([high, low], 1), 1, 1)[0:1]

    def as_column(row):
        at = lax.broadcasted_iota(jnp.int32, (TAIL, row.shape[1]), 0)
        high = row.astype(BF16).astype(F32)
        mid = (row - high).astype(BF16).astype(F32)
        low = row - high - mid
        stack = jnp.where(at == 0, high, jnp.where(at == 1, mid, jnp.where(at == 2, low, 0.0)))
        return matmul(stack.astype(BF16), ones_column, 0, 0)

    def exchange(phase, blk, terms):
        parts[phase, blk, member] = as_row(terms)

        def share(p, s):
            remote(
                parts.at[phase, blk, member],
                parts.at[phase, blk, member],
                x_send,
                x_recv.at[phase, blk],
                me_z * plane + p,
                s,
            ).start()

        peers(plane, me_p, share)

    def exchanged(phase, blk):
        if members > 1:
            whole = parts.at[phase, blk, pl.ds(0, members - 1)]
            pltpu.make_async_copy(whole, whole, x_recv.at[phase, blk]).wait()
        return jnp.sum(parts[phase, blk], axis=0)

    def layer_param(b, hh):
        at = hh * per_head
        tail = params[b, at, rows:, :].astype(F32)
        weight = params[b, at, :rows, :]
        if per_head > 1:
            for i in range(1, per_head):
                tail = tail + params[b, at + i, rows:, :].astype(F32)
            weight = jnp.concatenate(
                [params[b, at + i, :rows, :] for i in range(per_head)], axis=0
            )
        return weight, tail[0:1], tail[1:2]

    def layer_params(b):
        found = [layer_param(b, hh) for hh in range(heads)]
        return (
            diagonal([one[0] for one in found]),
            beside([one[1] for one in found], 1),
            beside([one[2] for one in found], 1),
        )

    at_row = lax.broadcasted_iota(jnp.int32, (seq, two), 0)
    at_col = lax.broadcasted_iota(jnp.int32, (seq, two), 1)
    first = at_col < seq
    allowed = at_row <= jnp.where(first, at_col, at_col - seq)
    wide_col = lax.broadcasted_iota(jnp.int32, (seq, hd), 1)
    wide_first = wide_col < seq
    wide_second = (wide_col >= seq) & (wide_col < two)
    vocab_lane = lax.broadcasted_iota(jnp.int32, (some, hd), 1).astype(F32)

    def wide(column):
        return beside([column] * heads, 1)

    def both(sides):
        return sides[:, :hd] if heads == 1 else sum(sides[:, lanes(hh)] for hh in range(heads))

    def embed(blk):
        for p in range(plane):
            col = as_column(toks[p, :, blk * some : (blk + 1) * some])
            picked = beside(
                [
                    jnp.where(vocab_lane + float(v * hd) == col, 1.0, 0.0).astype(BF16)
                    for v in range(vocab // hd)
                ],
                1,
            )
            found = matmul(picked, emb[...], 1, 0)
            at = slice(p * some, (p + 1) * some)
            xs[0, blk, at] = found[:, :held].astype(BF16)
            root = jnp.sum(found[:, held:], axis=1, keepdims=True)
            rstd[0, blk, at] = jnp.broadcast_to(root, (some, hd))

    def forward(b, blk):
        if b > 0:
            root = lax.rsqrt(exchanged(b - 1, blk) * (1.0 / width) + 1e-05)
            roots[b, blk] = root
            rstd[b, blk] = as_column(root)
        weight, gain_row, scale_row = layer_params(b)
        norm = (xs[b, blk].astype(F32) * wide(rstd[b, blk]) * gain_row).astype(BF16)
        normed[b, blk] = norm
        query = (matmul(norm, weight, 1, 0) * inv).astype(BF16)
        queries[b, blk] = query
        tiles = [(p, hh) for p in range(pairs) for hh in range(heads)]
        scores = []
        for p, hh in tiles:
            lo, mid, hi = p * two, p * two + seq, (p + 1) * two
            scores.append(
                matmul(
                    beside([norm[lo:mid, lanes(hh)], norm[mid:hi, lanes(hh)]], 1),
                    diagonal([query[lo:mid, lanes(hh)], query[mid:hi, lanes(hh)]]),
                    1,
                    1,
                )
            )
        spread = {}
        for (p, hh), score in zip(tiles, scores):
            score = jnp.where(allowed, score, -1e30)
            raised = jnp.exp(score - jnp.max(score, axis=0, keepdims=True))
            attend = raised * (1.0 / jnp.sum(raised, axis=0, keepdims=True))
            probs[b, blk, p, hh, :, 0:two] = attend
            if b + 1 < layers:
                spread[p, hh] = spread_out(attend)
        if b + 1 == layers:
            return
        terms = []
        for p in range(pairs):
            lo, hi = p * two, (p + 1) * two
            mix = mixed_rows(norm, spread, p)
            mixed[b, blk, lo:hi] = mix
            out_rows = (xs[b, blk, lo:hi].astype(F32) + scale_row * mix).astype(BF16)
            xs[b + 1, blk, lo:hi] = out_rows
            out_rows = out_rows.astype(F32)
            terms.append(both(out_rows * out_rows))
        exchange(b, blk, beside(terms, 0))

    def spread_out(attend):
        attend = attend.astype(BF16)
        zero = jnp.zeros_like(attend)
        return [jnp.where(first, attend, zero), jnp.where(first, zero, attend)]

    def mixed_rows(norm, spread, p):
        lo, hi = p * two, (p + 1) * two
        return matmul(
            beside([part for hh in range(heads) for part in spread[p, hh]], 0),
            diagonal([norm[lo:hi, lanes(hh)] for hh in range(heads)]),
            0,
            0,
        )

    def backward(b, blk):
        if b + 1 == layers:
            pltpu.make_async_copy(cot.at[blk], cot.at[blk], c_recv.at[blk]).wait()
        else:
            inner = exchanged(layers - 1 + b, blk) * (1.0 / width)
            root = roots[b + 1, blk]
            along = as_column(inner * root * root * root)
            _, gain_row, _ = layer_params(b + 1)
            dy = dnormed[blk].astype(F32) * gain_row
            back = wide(rstd[b + 1, blk]) * dy - xs[b + 1, blk].astype(F32) * wide(along)
        weight, gain_row, scale_row = layer_params(b)
        given = beside([cot[blk, hh] for hh in range(heads)], 1).astype(F32)
        if b + 1 < layers:
            given = (given + back).astype(BF16)
            if b > 0:
                for hh in range(heads):
                    cot[blk, hh] = given[:, lanes(hh)]
            given = given.astype(F32)
            add_tail(1, blk, jnp.sum(given * mixed[b, blk], axis=0, keepdims=True))
        dmix = (given * scale_row).astype(BF16)
        tiles = [(p, hh) for p in range(pairs) for hh in range(heads)]
        gap = jnp.zeros((hd - two, hd), BF16)
        wide_gap = jnp.zeros((hd - two, 2 * hd), BF16)
        datts = []
        for p, hh in tiles:
            lo, mid, hi = p * two, p * two + seq, (p + 1) * two
            datts.append(
                matmul(
                    beside(
                        [normed[b, blk, lo:mid, lanes(hh)], normed[b, blk, mid:hi, lanes(hh)]], 1
                    ),
                    beside(
                        [diagonal([dmix[lo:mid, lanes(hh)], dmix[mid:hi, lanes(hh)]]), wide_gap],
                        0,
                    ),
                    1,
                    1,
                )
            )
        dscores, attends = {}, {}
        for (p, hh), datt in zip(tiles, datts):
            datt = datt.astype(BF16).astype(F32)
            attend = probs[b, blk, p, hh]
            inner = jnp.sum(datt * attend, axis=0, keepdims=True)
            dscore = (attend * (datt - inner)).astype(BF16)
            attend = attend.astype(BF16)
            zero = jnp.zeros_like(dscore)
            dscores[p, hh] = beside(
                [jnp.where(wide_first, dscore, zero), jnp.where(wide_second, dscore, zero)], 0
            )
            attends[p, hh] = beside(
                [jnp.where(wide_first, attend, zero), jnp.where(wide_second, attend, zero)], 0
            )
        dqueries, dnorms = [], []
        for p in range(pairs):
            lo, hi = p * two, (p + 1) * two
            dquery = matmul(
                beside([dscores[p, hh] for hh in range(heads)], 0),
                diagonal([normed[b, blk, lo:hi, lanes(hh)] for hh in range(heads)]),
                0,
                0,
            )
            dqueries.append(dquery[:two].astype(BF16))
            dnorms.append(
                beside(
                    [
                        matmul(
                            beside([dscores[p, hh], attends[p, hh]], 1),
                            beside(
                                [
                                    queries[b, blk, lo:hi, lanes(hh)],
                                    gap,
                                    dmix[lo:hi, lanes(hh)],
                                    gap,
                                ],
                                0,
                            ),
                            1,
                            0,
                        )
                        for hh in range(heads)
                    ],
                    1,
                )
            )
        dquery = beside(dqueries, 0)

        if b == 0:
            for hh in range(heads):
                grad = matmul(normed[b, blk, :, lanes(hh)], dquery[:, lanes(hh)], 0, 0)
                if blk > 0:
                    grad = grad + grads[hh]
                grads[hh] = grad
            if blk + 1 == BLOCKS:
                send_grads(b)
        else:
            dqueried[blk] = dquery
        dnorm = beside(dnorms, 0) + matmul(dquery, weight, 1, 1) * inv
        dnorm = dnorm.astype(BF16)
        if b > 0:
            dnormed[blk] = dnorm
            x_in = xs[b, blk].astype(F32)
            exchange(layers - 2 + b, blk, both(dnorm.astype(F32) * gain_row * x_in))
        else:
            add_gain(b, blk, dnorm)
            if blk + 1 == BLOCKS:
                send_tails(b)

    def add_tail(row, blk, part):
        if blk > 0:
            part = part + tails[row : row + 1]
        tails[row : row + 1] = part

    def add_gain(b, blk, dnorm):
        unit = xs[b, blk].astype(F32) * wide(rstd[b, blk])
        add_tail(0, blk, jnp.sum(dnorm.astype(F32) * unit, axis=0, keepdims=True))

    def later_grads(b):
        for hh in range(heads):
            grads[hh] = matmul(
                beside([normed[b, blk, :, lanes(hh)] for blk in range(BLOCKS)], 0),
                beside([dqueried[blk, :, lanes(hh)] for blk in range(BLOCKS)], 0),
                0,
                0,
            )
        send_grads(b)

    def later_tails(b):
        for blk in range(BLOCKS):
            add_gain(b, blk, dnormed[blk])
            if b + 1 < layers:
                continue
            norm = normed[b, blk]
            spread = {
                (p, hh): spread_out(probs[b, blk, p, hh, :, 0:two])
                for p in range(pairs)
                for hh in range(heads)
            }
            mix = beside([mixed_rows(norm, spread, p) for p in range(pairs)], 0)
            given = beside([cot[blk, hh] for hh in range(heads)], 1).astype(F32)
            add_tail(1, blk, jnp.sum(given * mix, axis=0, keepdims=True))
        send_tails(b)

    def give_grads(b, source, target, sent, arrived):
        for hh in range(heads):
            for i in range(per_head):
                at = hh * per_head + i
                r = head_of(me_p, me_s, hh) * per_head + i
                mine = (r == me_d) & (me_s == b)

                @pl.when(mine)
                def _():
                    pltpu.make_async_copy(source.at[b, at], target.at[me_z], arrived).start()

                @pl.when(jnp.logical_not(mine))
                def _():
                    remote(source.at[b, at], target.at[me_z], sent, arrived, r, b).start()

    def send_grads(b):
        for hh in range(heads):
            dweight = (grads[hh] * inv).astype(BF16)
            for i in range(per_head):
                tx[b, hh * per_head + i] = dweight[i * rows : (i + 1) * rows]
        give_grads(b, tx, rx, g_send, g_recv)

    def send_tails(b):
        for hh in range(heads):
            gain_part, scale_part = tails[0:1, lanes(hh)], tails[1:2, lanes(hh)]
            gain_hi = gain_part.astype(BF16).astype(F32)
            scale_hi = scale_part.astype(BF16).astype(F32)
            tail = jnp.where(
                tail_row == 0,
                gain_hi,
                jnp.where(
                    tail_row == 1,
                    gain_part - gain_hi,
                    jnp.where(
                        tail_row == 2,
                        scale_hi,
                        jnp.where(tail_row == 3, scale_part - scale_hi, 0.0),
                    ),
                ),
            ).astype(BF16)
            for i in range(per_head):
                tail_tx[b, hh * per_head + i] = tail
        give_grads(b, tail_tx, tail_rx, tg_send, tg_recv)

    pltpu.make_async_copy(tbl, tbl, load_sem).wait()
    chunk = math.gcd(vocab, 128)
    lane_chunk = lax.broadcasted_iota(jnp.int32, (chunk, hd), 1)

    def table_norm(i, carry):
        at = pl.ds(pl.multiple_of(i * chunk, chunk), chunk)
        squares = jnp.zeros((chunk, hd), F32)
        for h in range(width // hd):
            block = tbl[at, h * hd : (h + 1) * hd].astype(F32)
            squares = squares + block * block
        root = lax.rsqrt(jnp.sum(squares, axis=1, keepdims=True) * (1.0 / width) + 1e-05)
        high = root.astype(BF16).astype(F32)
        mid = (root - high).astype(BF16).astype(F32)
        low = root - high - mid
        emb[at, held : held + hd] = jnp.where(
            lane_chunk == 0,
            high,
            jnp.where(lane_chunk == 1, mid, jnp.where(lane_chunk == 2, low, 0.0)),
        ).astype(BF16)
        return carry

    lax.fori_loop(0, vocab // chunk, table_norm, 0)

    for load in own_columns:
        load.wait()
    if plane > 1:
        pltpu.make_async_copy(
            toks.at[pl.ds(0, plane - 1)], toks.at[pl.ds(0, plane - 1)], t_recv
        ).wait()
    embed(0)
    for b in range(layers):
        pltpu.make_async_copy(params.at[b], params.at[b], w_recv.at[b]).wait()
        for blk in range(BLOCKS):
            if b == 0 and blk > 0:
                embed(blk)
            forward(b, blk)
            if b == 0 and blk + 1 < BLOCKS:
                send_cot(blk + 1)
            if b + 1 == layers:
                backward(b, blk)
    for b in reversed(range(layers - 1)):
        later_grads(b + 1)
        later_tails(b + 1)
        for blk in range(BLOCKS):
            backward(b, blk)

    pltpu.make_async_copy(rx, rx, g_recv).wait()
    total_query = jnp.sum(rx[...].astype(F32), axis=0)
    query_squares = jnp.sum(total_query * total_query, axis=0, keepdims=True)
    pltpu.make_async_copy(tail_rx, tail_rx, tg_recv).wait()
    total = jnp.sum(tail_rx[...].astype(F32), axis=0)
    total_gain = total[0:1] + total[1:2]
    total_scale = total[2:3] + total[3:4]
    if per_head > 1:
        at = lax.broadcasted_iota(jnp.int32, (1, hd), 1)
        start = lax.rem(me_d, per_head) * rows
        inside = (at >= start) & (at < start + rows)
        total_gain = jnp.where(inside, total_gain, 0.0)
        total_scale = jnp.where(inside, total_scale, 0.0)
    squares = (
        query_squares
        + total_gain * total_gain
        + total_scale * total_scale
    )
    norms[pl.ds(me, 1)] = squares[None]

    def tell(d, s):
        remote(norms.at[me], norms.at[me], n_send, n_recv, d, s).start()

    peers(n_dp, me_d, tell)

    if members > 1:
        for phase in range(2 * layers - 2):
            whole = parts.at[phase, :, pl.ds(0, members - 1)]
            pltpu.make_async_copy(whole, whole, x_send).wait()
    if plane > 1:
        sent = toks.at[pl.ds(0, plane - 1)]
        pltpu.make_async_copy(sent, sent, t_send).wait()
        sent = cot.at[:, :, pl.ds(0, (plane - 1) * some)]
        pltpu.make_async_copy(sent, sent, c_send).wait()

    def sent_weight(k, carry):
        pltpu.make_async_copy(packed, packed, w_send).wait()
        return carry

    lax.fori_loop(0, jnp.where(keep, planes - 1, planes), sent_weight, 0)

    def sent_grad(k, carry):
        pltpu.make_async_copy(rx.at[0], rx.at[0], g_send).wait()
        pltpu.make_async_copy(tail_rx.at[0], tail_rx.at[0], tg_send).wait()
        return carry

    pieces = layers * heads * per_head
    lax.fori_loop(0, jnp.where(keep, pieces - 1, pieces), sent_grad, 0)

    others = norms.at[pl.ds(0, n_dev - 1)]
    pltpu.make_async_copy(others, others, n_recv).wait()
    overall = jnp.sum(jnp.sum(norms[...], axis=0), axis=1, keepdims=True)
    limit = float(layers * width * (hd + 2))
    factor = jnp.minimum(1.0, math.sqrt(limit) / jnp.sqrt(overall))
    out[0:rows] = total_query * factor
    out[rows : rows + 8] = jnp.where(
        lax.broadcasted_iota(jnp.int32, (8, hd), 0) == 0, total_gain * factor, total_scale * factor
    )
    pltpu.make_async_copy(others, others, n_send).wait()


def split_kernel(found, query_grad, gain_grad, scale_grad):
    rows = query_grad.shape[0]
    query_grad[...] = found[0:rows]
    gain_grad[...] = found[rows : rows + 1]
    scale_grad[...] = found[rows + 1 : rows + 2]


def on_device(path_table, tokens, assign, out_grad, query_weights, gain, scale):
    n_dp = lax.axis_size("dp")
    n_sec = lax.axis_size("section")
    vocab, width = path_table.shape
    slots, seq = tokens.shape[1:]
    rows, hd = query_weights.shape[1:]
    count = slots * seq
    layers = n_sec
    plane, planes, heads = layout(n_dp, n_sec, width, hd)
    per_head = hd // rows
    pieces = heads * per_head
    n_dev = n_dp * n_sec
    held = heads * hd
    block_rows = plane * count // BLOCKS
    pairs = block_rows // (2 * seq)
    phases = max(1, 2 * layers - 2)
    first = lax.rem(lax.axis_index("dp") * rows, hd)
    if rows < hd:
        gain = lax.dynamic_update_slice(jnp.zeros((1, hd), BF16), gain, (0, first))
        scale = lax.dynamic_update_slice(jnp.zeros((1, hd), BF16), scale, (0, first))
    vmem = pl.BlockSpec(memory_space=pltpu.VMEM)
    hbm = pl.BlockSpec(memory_space=pl.ANY)
    stream = pltpu.VMEM((layers, BLOCKS, block_rows, held), BF16)
    found = pl.pallas_call(
        functools.partial(step_kernel, n_dp, n_sec),
        out_shape=pltpu.VMEM((rows + 8, hd), F32),
        in_specs=[hbm] * 7,
        out_specs=vmem,
        scratch_shapes=[
            pltpu.VMEM((slots, seq), jnp.int32),
            pltpu.SMEM((slots,), jnp.int32),
            pltpu.VMEM((1, hd), BF16),
            pltpu.VMEM((1, hd), BF16),
            pltpu.VMEM((rows + TAIL, hd), BF16),
            pltpu.VMEM((layers, pieces, rows + TAIL, hd), BF16),
            pltpu.VMEM((plane, 1, count), F32),
            pltpu.VMEM((vocab, width), BF16),
            pltpu.VMEM((vocab, held + hd), BF16),
            pltpu.VMEM((BLOCKS, heads, block_rows, hd), BF16),
            stream,
            stream,
            stream,
            pltpu.VMEM((layers, BLOCKS, block_rows, held), F32),
            pltpu.VMEM((layers, BLOCKS, pairs, heads, seq, hd), F32),
            pltpu.VMEM((BLOCKS, block_rows, held), BF16),
            pltpu.VMEM((BLOCKS, block_rows, held), BF16),
            pltpu.VMEM((layers, BLOCKS, block_rows, hd), F32),
            pltpu.VMEM((layers, BLOCKS, 1, block_rows), F32),
            pltpu.VMEM((phases, BLOCKS, plane * n_sec, 1, block_rows), F32),
            pltpu.VMEM((heads, hd, hd), F32),
            pltpu.VMEM((8, held), F32),
            pltpu.VMEM((layers, pieces, rows, hd), BF16),
            pltpu.VMEM((planes, rows, hd), BF16),
            pltpu.VMEM((layers, pieces, TAIL, hd), BF16),
            pltpu.VMEM((planes, TAIL, hd), BF16),
            pltpu.VMEM((n_dev, 1, hd), F32),
            pltpu.SemaphoreType.DMA((5,)),
            pltpu.SemaphoreType.DMA,
            pltpu.SemaphoreType.DMA((heads,)),
            pltpu.SemaphoreType.DMA,
            pltpu.SemaphoreType.DMA,
            pltpu.SemaphoreType.DMA,
            pltpu.SemaphoreType.DMA((layers,)),
            pltpu.SemaphoreType.DMA,
            pltpu.SemaphoreType.DMA((BLOCKS,)),
            pltpu.SemaphoreType.DMA,
            pltpu.SemaphoreType.DMA((phases, BLOCKS)),
            pltpu.SemaphoreType.DMA,
            pltpu.SemaphoreType.DMA,
            pltpu.SemaphoreType.DMA,
            pltpu.SemaphoreType.DMA,
            pltpu.SemaphoreType.DMA,
            pltpu.SemaphoreType.DMA,
        ],
        compiler_params=pltpu.CompilerParams(
            collective_id=0, has_side_effects=True, vmem_limit_bytes=56 * 1024 * 1024
        ),
    )(
        path_table,
        tokens[0],
        assign[0],
        out_grad.reshape(count, width),
        query_weights[0],
        gain,
        scale,
    )
    query_grad, gain_grad, scale_grad = pl.pallas_call(
        split_kernel,
        out_shape=(
            jax.ShapeDtypeStruct((rows, hd), F32),
            jax.ShapeDtypeStruct((1, hd), F32),
            jax.ShapeDtypeStruct((1, hd), F32),
        ),
        in_specs=[vmem],
        out_specs=(vmem, vmem, vmem),
        compiler_params=pltpu.CompilerParams(vmem_limit_bytes=1024 * 1024),
    )(found)
    if rows < hd:
        gain_grad = lax.dynamic_slice(gain_grad, (0, first), (1, rows))
        scale_grad = lax.dynamic_slice(scale_grad, (0, first), (1, rows))
    return query_grad[None], gain_grad, scale_grad


def solution(mesh):
    in_specs = (
        P(),
        P("dp", None, None),
        P("dp", None),
        P("dp", None, None, None, None),
        P("section", "dp", None),
        P("section", "dp"),
        P("section", "dp"),
    )
    out_specs = (P("section", "dp", None), P("section", "dp"), P("section", "dp"))
    return jax.shard_map(
        on_device, mesh=mesh, in_specs=in_specs, out_specs=out_specs, check_vma=False
    )
```

```python
import functools
import math

import jax
import jax.numpy as jnp
from jax import lax
from jax.experimental import pallas as pl
from jax.experimental.pallas import tpu as pltpu
from jax.sharding import PartitionSpec as P

MESH = pl.DeviceIdType.MESH
F32 = jnp.float32
BF16 = jnp.bfloat16
TAIL = 16
PLANE = 4
BLOCKS = 2
SHARES = (1, 1, 2)
UNROLL = 32


def matmul(lhs, rhs, lhs_dim, rhs_dim):
    return lax.dot_general(
        lhs, rhs, (((lhs_dim,), (rhs_dim,)), ((), ())), preferred_element_type=F32
    )


def beside(parts, axis):
    return parts[0] if len(parts) == 1 else jnp.concatenate(parts, axis=axis)


def diagonal(parts):
    zero = jnp.zeros_like(parts[0])
    return beside(
        [
            beside([part if i == k else zero for k in range(len(parts))], 1)
            for i, part in enumerate(parts)
        ],
        0,
    )


def layout(n_dp, n_sec, width, hd):
    plane = math.gcd(n_dp, min(PLANE, width // hd // n_sec))
    return plane, n_dp // plane, width // hd // n_sec // plane


def step_kernel(
    n_dp,
    n_sec,
    table,
    tokens,
    assign,
    out_grad,
    weights,
    gain,
    scale,
    out,
    tokens_in,
    assign_in,
    gain_in,
    scale_in,
    packed,
    params,
    toks,
    tbl,
    emb,
    picked,
    table_rstd,
    cot,
    xs,
    normed,
    queries,
    mixed,
    probs,
    dnormed,
    dqueried,
    rstd,
    roots,
    parts,
    grads,
    tails,
    tx,
    rx,
    tail_tx,
    tail_rx,
    norms,
    in_sem,
    load_sem,
    emb_sem,
    t_send,
    t_recv,
    w_send,
    w_recv,
    c_send,
    c_recv,
    x_send,
    x_recv,
    g_send,
    g_recv,
    tg_send,
    tg_recv,
    n_send,
    n_recv,
):
    slots, seq = tokens.shape
    vocab, width = table.shape
    rows, hd = weights.shape
    plane, planes, heads = layout(n_dp, n_sec, width, hd)
    layers = n_sec
    per_head = hd // rows
    n_dev = n_dp * n_sec
    members = plane * n_sec
    held = heads * hd
    some = slots // BLOCKS * seq
    block_rows = plane * some
    two = 2 * seq
    pairs = block_rows // two
    inv = 1.0 / math.sqrt(hd)
    me_d = lax.axis_index("dp")
    me_s = lax.axis_index("section")
    me = me_d * n_sec + me_s
    me_z = lax.div(me_d, plane)
    me_p = lax.rem(me_d, plane)
    member = me_p * n_sec + me_s

    def repeat(first, last, body):
        if last - first <= UNROLL:
            for k in range(first, last):
                body(k)
        else:

            def step(k, carry):
                body(k)
                return carry

            lax.fori_loop(first, last, step, 0)

    def after(at, k, size):
        moved = at + k
        return jnp.where(moved >= size, moved - size, moved)

    def peers(size, at, body):
        if size * n_sec <= UNROLL:
            for kd in range(size):
                d = after(at, kd, size) if kd else at
                for ks in range(n_sec):
                    if kd or ks:
                        body(d, after(me_s, ks, n_sec) if ks else me_s)
        else:

            def step(k, carry):
                t = lax.rem(at * n_sec + me_s + k, size * n_sec)
                body(lax.div(t, n_sec), lax.rem(t, n_sec))
                return carry

            lax.fori_loop(1, size * n_sec, step, 0)

    def head_of(p, c, hh):
        return (c * heads + hh) * plane + p

    def columns(h):
        return pl.ds(pl.multiple_of(h * hd, hd), hd)

    def lanes(hh):
        return slice(hh * hd, (hh + 1) * hd)

    def remote(src, dst, ssem, rsem, d, s):
        return pltpu.make_async_remote_copy(
            src_ref=src,
            dst_ref=dst,
            send_sem=ssem,
            recv_sem=rsem,
            device_id=(d, s),
            device_id_type=MESH,
        )

    barrier = pltpu.get_barrier_semaphore()

    def greet(d, s):
        pl.semaphore_signal(barrier, inc=1, device_id=(d, s), device_id_type=MESH)

    peers(n_dp, me_d, greet)
    pltpu.make_async_copy(table, tbl, load_sem).start()
    loads = [
        pltpu.make_async_copy(tokens, tokens_in, in_sem.at[0]),
        pltpu.make_async_copy(assign, assign_in, in_sem.at[1]),
        pltpu.make_async_copy(weights, packed.at[pl.ds(0, rows)], in_sem.at[2]),
        pltpu.make_async_copy(gain, gain_in, in_sem.at[3]),
        pltpu.make_async_copy(scale, scale_in, in_sem.at[4]),
    ]
    for load in loads:
        load.start()
    own_columns = [
        pltpu.make_async_copy(
            table.at[:, columns(head_of(me_p, me_s, hh))], emb.at[:, lanes(hh)], emb_sem.at[hh]
        )
        for hh in range(heads)
    ]
    for load in own_columns:
        load.start()

    def cot_at(blk, p, hh, start, size):
        return cot.at[blk, hh, pl.ds(p * some + start, size)]

    def cot_from(blk, h, start, size):
        return out_grad.at[pl.ds(blk * some + start, size), columns(h)]

    for blk in range(BLOCKS):
        for hh in range(heads):
            pltpu.make_async_copy(
                cot_from(blk, head_of(me_p, me_s, hh), 0, some),
                cot_at(blk, me_p, hh, 0, some),
                c_recv.at[blk],
            ).start()

    for load in loads:
        load.wait()
    tail_row = lax.broadcasted_iota(jnp.int32, (TAIL, hd), 0)
    packed[rows : rows + TAIL, :] = jnp.where(
        tail_row == 0,
        gain_in[...].astype(F32),
        jnp.where(tail_row == 1, scale_in[...].astype(F32), 0.0),
    ).astype(BF16)
    toks[me_p] = beside(
        [tokens_in[pl.ds(assign_in[j], 1), :].astype(F32) for j in range(slots)], 1
    )
    probs[...] = jnp.zeros(probs.shape, F32)

    pl.semaphore_wait(barrier, n_dev - 1)

    my_head = lax.div(me_d * rows, hd)
    to_p = lax.rem(my_head, plane)
    to_i = lax.div(my_head, plane)
    to_s = lax.div(to_i, heads)
    place = lax.rem(to_i, heads) * per_head + lax.rem(me_d, per_head)
    keep = (to_p == me_p) & (to_s == me_s)

    def give(k):
        z = lax.rem(me_z + k, planes)
        remote(
            packed, params.at[me_s, place], w_send, w_recv.at[me_s], z * plane + to_p, to_s
        ).start()

    repeat(1, planes, give)
    for k in range(1, plane):
        p = lax.rem(me_p + k, plane)
        remote(toks.at[me_p], toks.at[me_p], t_send, t_recv, me_z * plane + p, me_s).start()

    @pl.when(keep)
    def _():
        pltpu.make_async_copy(packed, params.at[me_s, place], w_recv.at[me_s]).start()

    @pl.when(jnp.logical_not(keep))
    def _():
        remote(
            packed,
            params.at[me_s, place],
            w_send,
            w_recv.at[me_s],
            me_z * plane + to_p,
            to_s,
        ).start()

    cuts = [sum(SHARES[:k]) * some // sum(SHARES) for k in range(len(SHARES) + 1)]

    def send_cot(blk, begin, end):
        if begin == end:
            return
        for k in range(1, plane):
            p = lax.rem(me_p + k, plane)
            for hh in range(heads):
                remote(
                    cot_from(blk, head_of(p, me_s, hh), begin, end - begin),
                    cot_at(blk, me_p, hh, begin, end - begin),
                    c_send,
                    c_recv.at[blk],
                    me_z * plane + p,
                    me_s,
                ).start()

    for blk in range(BLOCKS - 1):
        send_cot(blk, 0, some)
    send_cot(BLOCKS - 1, cuts[0], cuts[1])

    ones_row = jnp.ones((TAIL, 2 * hd), BF16)
    ones_column = jnp.ones((TAIL, hd), BF16)

    def as_row(terms):
        high = terms.astype(BF16)
        low = (terms - high.astype(F32)).astype(BF16)
        return matmul(ones_row, beside([high, low], 1), 1, 1)[0:1]

    def as_column(row):
        at = lax.broadcasted_iota(jnp.int32, (TAIL, row.shape[1]), 0)
        high = row.astype(BF16).astype(F32)
        mid = (row - high).astype(BF16).astype(F32)
        low = row - high - mid
        stack = jnp.where(at == 0, high, jnp.where(at == 1, mid, jnp.where(at == 2, low, 0.0)))
        return matmul(stack.astype(BF16), ones_column, 0, 0)

    def exchange(phase, blk, terms):
        parts[phase, blk, member] = as_row(terms)

        def share(p, s):
            remote(
                parts.at[phase, blk, member],
                parts.at[phase, blk, member],
                x_send,
                x_recv.at[phase, blk],
                me_z * plane + p,
                s,
            ).start()

        peers(plane, me_p, share)

    def exchanged(phase, blk):
        if members > 1:
            whole = parts.at[phase, blk, pl.ds(0, members - 1)]
            pltpu.make_async_copy(whole, whole, x_recv.at[phase, blk]).wait()
        return jnp.sum(parts[phase, blk], axis=0)

    def layer_param(b, hh):
        at = hh * per_head
        tail = params[b, at, rows:, :].astype(F32)
        weight = params[b, at, :rows, :]
        if per_head > 1:
            for i in range(1, per_head):
                tail = tail + params[b, at + i, rows:, :].astype(F32)
            weight = jnp.concatenate(
                [params[b, at + i, :rows, :] for i in range(per_head)], axis=0
            )
        return weight, tail[0:1], tail[1:2]

    def layer_params(b):
        found = [layer_param(b, hh) for hh in range(heads)]
        return (
            diagonal([one[0] for one in found]),
            beside([one[1] for one in found], 1),
            beside([one[2] for one in found], 1),
        )

    at_row = lax.broadcasted_iota(jnp.int32, (seq, two), 0)
    at_col = lax.broadcasted_iota(jnp.int32, (seq, two), 1)
    first = at_col < seq
    allowed = at_row <= jnp.where(first, at_col, at_col - seq)
    wide_col = lax.broadcasted_iota(jnp.int32, (seq, hd), 1)
    wide_first = wide_col < seq
    wide_second = (wide_col >= seq) & (wide_col < two)
    vocab_lane = lax.broadcasted_iota(jnp.int32, (some, hd), 1).astype(F32)

    def wide(column):
        return beside([column] * heads, 1)

    def both(sides):
        return sides[:, :hd] if heads == 1 else sum(sides[:, lanes(hh)] for hh in range(heads))

    def embed(blk):
        for p in range(plane):
            col = as_column(toks[p, :, blk * some : (blk + 1) * some])
            at = slice(p * some, (p + 1) * some)
            root = jnp.zeros((some, hd), F32)
            for v in range(vocab // hd):
                hit = vocab_lane + float(v * hd) == col
                picked[at, lanes(v)] = jnp.where(hit, 1.0, 0.0).astype(BF16)
                root = root + jnp.where(hit, table_rstd[:, lanes(v)], 0.0)
            rstd[0, blk, at] = jnp.broadcast_to(jnp.sum(root, axis=1, keepdims=True), (some, hd))
        xs[0, blk] = matmul(picked[...], emb[...], 1, 0).astype(BF16)

    def forward(b, blk):
        if b > 0:
            root = lax.rsqrt(exchanged(b - 1, blk) * (1.0 / width) + 1e-05)
            roots[b, blk] = root
            rstd[b, blk] = as_column(root)
        weight, gain_row, scale_row = layer_params(b)
        norm = (xs[b, blk].astype(F32) * wide(rstd[b, blk]) * gain_row).astype(BF16)
        normed[b, blk] = norm
        query = (matmul(norm, weight, 1, 0) * inv).astype(BF16)
        queries[b, blk] = query
        tiles = [(p, hh) for p in range(pairs) for hh in range(heads)]
        scores = []
        for p, hh in tiles:
            lo, mid, hi = p * two, p * two + seq, (p + 1) * two
            scores.append(
                matmul(
                    beside([norm[lo:mid, lanes(hh)], norm[mid:hi, lanes(hh)]], 1),
                    diagonal([query[lo:mid, lanes(hh)], query[mid:hi, lanes(hh)]]),
                    1,
                    1,
                )
            )
        spread = {}
        for (p, hh), score in zip(tiles, scores):
            score = jnp.where(allowed, score, -1e30)
            raised = jnp.exp(score - jnp.max(score, axis=0, keepdims=True))
            attend = raised * (1.0 / jnp.sum(raised, axis=0, keepdims=True))
            probs[b, blk, p, hh, :, 0:two] = attend
            if b + 1 < layers:
                spread[p, hh] = spread_out(attend)
        if b + 1 == layers:
            return
        terms = []
        for p in range(pairs):
            lo, hi = p * two, (p + 1) * two
            mix = mixed_rows(norm, spread, p)
            mixed[b, blk, lo:hi] = mix
            out_rows = (xs[b, blk, lo:hi].astype(F32) + scale_row * mix).astype(BF16)
            xs[b + 1, blk, lo:hi] = out_rows
            out_rows = out_rows.astype(F32)
            terms.append(both(out_rows * out_rows))
        exchange(b, blk, beside(terms, 0))

    def spread_out(attend):
        attend = attend.astype(BF16)
        zero = jnp.zeros_like(attend)
        return [jnp.where(first, attend, zero), jnp.where(first, zero, attend)]

    def mixed_rows(norm, spread, p):
        lo, hi = p * two, (p + 1) * two
        return matmul(
            beside([part for hh in range(heads) for part in spread[p, hh]], 0),
            diagonal([norm[lo:hi, lanes(hh)] for hh in range(heads)]),
            0,
            0,
        )

    def backward(b, blk):
        if b + 1 == layers:
            pltpu.make_async_copy(cot.at[blk], cot.at[blk], c_recv.at[blk]).wait()
        else:
            inner = exchanged(layers - 1 + b, blk) * (1.0 / width)
            root = roots[b + 1, blk]
            along = as_column(inner * root * root * root)
            _, gain_row, _ = layer_params(b + 1)
            dy = dnormed[blk].astype(F32) * gain_row
            back = wide(rstd[b + 1, blk]) * dy - xs[b + 1, blk].astype(F32) * wide(along)
        weight, gain_row, scale_row = layer_params(b)
        given = beside([cot[blk, hh] for hh in range(heads)], 1).astype(F32)
        if b + 1 < layers:
            given = (given + back).astype(BF16)
            if b > 0:
                for hh in range(heads):
                    cot[blk, hh] = given[:, lanes(hh)]
            given = given.astype(F32)
            add_tail(1, blk, jnp.sum(given * mixed[b, blk], axis=0, keepdims=True))
        dmix = (given * scale_row).astype(BF16)
        tiles = [(p, hh) for p in range(pairs) for hh in range(heads)]
        gap = jnp.zeros((hd - two, hd), BF16)
        wide_gap = jnp.zeros((hd - two, 2 * hd), BF16)
        datts = []
        for p, hh in tiles:
            lo, mid, hi = p * two, p * two + seq, (p + 1) * two
            datts.append(
                matmul(
                    beside(
                        [normed[b, blk, lo:mid, lanes(hh)], normed[b, blk, mid:hi, lanes(hh)]], 1
                    ),
                    beside(
                        [diagonal([dmix[lo:mid, lanes(hh)], dmix[mid:hi, lanes(hh)]]), wide_gap],
                        0,
                    ),
                    1,
                    1,
                )
            )
        dscores, attends = {}, {}
        for (p, hh), datt in zip(tiles, datts):
            datt = datt.astype(BF16).astype(F32)
            attend = probs[b, blk, p, hh]
            inner = jnp.sum(datt * attend, axis=0, keepdims=True)
            dscore = (attend * (datt - inner)).astype(BF16)
            attend = attend.astype(BF16)
            zero = jnp.zeros_like(dscore)
            dscores[p, hh] = beside(
                [jnp.where(wide_first, dscore, zero), jnp.where(wide_second, dscore, zero)], 0
            )
            attends[p, hh] = beside(
                [jnp.where(wide_first, attend, zero), jnp.where(wide_second, attend, zero)], 0
            )
        dqueries, dnorms = [], []
        for p in range(pairs):
            lo, hi = p * two, (p + 1) * two
            dquery = matmul(
                beside([dscores[p, hh] for hh in range(heads)], 0),
                diagonal([normed[b, blk, lo:hi, lanes(hh)] for hh in range(heads)]),
                0,
                0,
            )
            dqueries.append(dquery[:two].astype(BF16))
            dnorms.append(
                beside(
                    [
                        matmul(
                            beside([dscores[p, hh], attends[p, hh]], 1),
                            beside(
                                [
                                    queries[b, blk, lo:hi, lanes(hh)],
                                    gap,
                                    dmix[lo:hi, lanes(hh)],
                                    gap,
                                ],
                                0,
                            ),
                            1,
                            0,
                        )
                        for hh in range(heads)
                    ],
                    1,
                )
            )
        dquery = beside(dqueries, 0)

        if b == 0:
            for hh in range(heads):
                grad = matmul(normed[b, blk, :, lanes(hh)], dquery[:, lanes(hh)], 0, 0)
                if blk > 0:
                    grad = grad + grads[hh]
                grads[hh] = grad
            if blk + 1 == BLOCKS:
                send_grads(b)
        else:
            dqueried[blk] = dquery
        dnorm = beside(dnorms, 0) + matmul(dquery, weight, 1, 1) * inv
        dnorm = dnorm.astype(BF16)
        if b > 0:
            dnormed[blk] = dnorm
            x_in = xs[b, blk].astype(F32)
            exchange(layers - 2 + b, blk, both(dnorm.astype(F32) * gain_row * x_in))
        else:
            add_gain(b, blk, dnorm)
            if blk + 1 == BLOCKS:
                send_tails(b)

    def add_tail(row, blk, part):
        if blk > 0:
            part = part + tails[row : row + 1]
        tails[row : row + 1] = part

    def add_gain(b, blk, dnorm):
        unit = xs[b, blk].astype(F32) * wide(rstd[b, blk])
        add_tail(0, blk, jnp.sum(dnorm.astype(F32) * unit, axis=0, keepdims=True))

    def later_grads(b):
        for hh in range(heads):
            grads[hh] = matmul(
                beside([normed[b, blk, :, lanes(hh)] for blk in range(BLOCKS)], 0),
                beside([dqueried[blk, :, lanes(hh)] for blk in range(BLOCKS)], 0),
                0,
                0,
            )
        send_grads(b)

    def later_tails(b):
        for blk in range(BLOCKS):
            add_gain(b, blk, dnormed[blk])
            if b + 1 < layers:
                continue
            norm = normed[b, blk]
            spread = {
                (p, hh): spread_out(probs[b, blk, p, hh, :, 0:two])
                for p in range(pairs)
                for hh in range(heads)
            }
            mix = beside([mixed_rows(norm, spread, p) for p in range(pairs)], 0)
            given = beside([cot[blk, hh] for hh in range(heads)], 1).astype(F32)
            add_tail(1, blk, jnp.sum(given * mix, axis=0, keepdims=True))
        send_tails(b)

    def give_grads(b, source, target, sent, arrived):
        for hh in range(heads):
            for i in range(per_head):
                at = hh * per_head + i
                r = head_of(me_p, me_s, hh) * per_head + i
                mine = (r == me_d) & (me_s == b)

                @pl.when(mine)
                def _():
                    pltpu.make_async_copy(source.at[b, at], target.at[me_z], arrived).start()

                @pl.when(jnp.logical_not(mine))
                def _():
                    remote(source.at[b, at], target.at[me_z], sent, arrived, r, b).start()

    def send_grads(b):
        for hh in range(heads):
            dweight = (grads[hh] * inv).astype(BF16)
            for i in range(per_head):
                tx[b, hh * per_head + i] = dweight[i * rows : (i + 1) * rows]
        give_grads(b, tx, rx, g_send, g_recv)

    def send_tails(b):
        for hh in range(heads):
            gain_part, scale_part = tails[0:1, lanes(hh)], tails[1:2, lanes(hh)]
            gain_hi = gain_part.astype(BF16).astype(F32)
            scale_hi = scale_part.astype(BF16).astype(F32)
            tail = jnp.where(
                tail_row == 0,
                gain_hi,
                jnp.where(
                    tail_row == 1,
                    gain_part - gain_hi,
                    jnp.where(
                        tail_row == 2,
                        scale_hi,
                        jnp.where(tail_row == 3, scale_part - scale_hi, 0.0),
                    ),
                ),
            ).astype(BF16)
            for i in range(per_head):
                tail_tx[b, hh * per_head + i] = tail
        give_grads(b, tail_tx, tail_rx, tg_send, tg_recv)

    pltpu.make_async_copy(tbl, tbl, load_sem).wait()
    chunk = math.gcd(vocab, 128)

    def table_norm(i, carry):
        at = pl.ds(pl.multiple_of(i * chunk, chunk), chunk)
        squares = jnp.zeros((chunk, hd), F32)
        for h in range(width // hd):
            block = tbl[at, h * hd : (h + 1) * hd].astype(F32)
            squares = squares + block * block
        table_rstd[:, at] = lax.rsqrt(as_row(squares) * (1.0 / width) + 1e-05)
        return carry

    lax.fori_loop(0, vocab // chunk, table_norm, 0)

    for load in own_columns:
        load.wait()
    if plane > 1:
        pltpu.make_async_copy(
            toks.at[pl.ds(0, plane - 1)], toks.at[pl.ds(0, plane - 1)], t_recv
        ).wait()
    embed(0)
    for b in range(layers):
        pltpu.make_async_copy(params.at[b], params.at[b], w_recv.at[b]).wait()
        for blk in range(BLOCKS):
            if b == 0 and blk > 0:
                embed(blk)
            forward(b, blk)
            if b == 0:
                send_cot(BLOCKS - 1, cuts[blk + 1], cuts[blk + 2])
            if b + 1 == layers:
                backward(b, blk)
    for b in reversed(range(layers - 1)):
        later_grads(b + 1)
        later_tails(b + 1)
        for blk in range(BLOCKS):
            backward(b, blk)

    pltpu.make_async_copy(rx, rx, g_recv).wait()
    total_query = jnp.sum(rx[...].astype(F32), axis=0)
    query_squares = jnp.sum(total_query * total_query, axis=0, keepdims=True)
    pltpu.make_async_copy(tail_rx, tail_rx, tg_recv).wait()
    total = jnp.sum(tail_rx[...].astype(F32), axis=0)
    total_gain = total[0:1] + total[1:2]
    total_scale = total[2:3] + total[3:4]
    if per_head > 1:
        at = lax.broadcasted_iota(jnp.int32, (1, hd), 1)
        start = lax.rem(me_d, per_head) * rows
        inside = (at >= start) & (at < start + rows)
        total_gain = jnp.where(inside, total_gain, 0.0)
        total_scale = jnp.where(inside, total_scale, 0.0)
    squares = (
        query_squares
        + total_gain * total_gain
        + total_scale * total_scale
    )
    norms[pl.ds(me, 1)] = squares[None]

    def tell(d, s):
        remote(norms.at[me], norms.at[me], n_send, n_recv, d, s).start()

    peers(n_dp, me_d, tell)

    if members > 1:
        for phase in range(2 * layers - 2):
            whole = parts.at[phase, :, pl.ds(0, members - 1)]
            pltpu.make_async_copy(whole, whole, x_send).wait()
    if plane > 1:
        sent = toks.at[pl.ds(0, plane - 1)]
        pltpu.make_async_copy(sent, sent, t_send).wait()
        sent = cot.at[:, :, pl.ds(0, (plane - 1) * some)]
        pltpu.make_async_copy(sent, sent, c_send).wait()

    def sent_weight(k, carry):
        pltpu.make_async_copy(packed, packed, w_send).wait()
        return carry

    lax.fori_loop(0, jnp.where(keep, planes - 1, planes), sent_weight, 0)

    def sent_grad(k, carry):
        pltpu.make_async_copy(rx.at[0], rx.at[0], g_send).wait()
        pltpu.make_async_copy(tail_rx.at[0], tail_rx.at[0], tg_send).wait()
        return carry

    pieces = layers * heads * per_head
    lax.fori_loop(0, jnp.where(keep, pieces - 1, pieces), sent_grad, 0)

    others = norms.at[pl.ds(0, n_dev - 1)]
    pltpu.make_async_copy(others, others, n_recv).wait()
    overall = jnp.sum(jnp.sum(norms[...], axis=0), axis=1, keepdims=True)
    limit = float(layers * width * (hd + 2))
    factor = jnp.minimum(1.0, math.sqrt(limit) / jnp.sqrt(overall))
    out[0:rows] = total_query * factor
    out[rows : rows + 8] = jnp.where(
        lax.broadcasted_iota(jnp.int32, (8, hd), 0) == 0, total_gain * factor, total_scale * factor
    )
    pltpu.make_async_copy(others, others, n_send).wait()


def split_kernel(found, query_grad, gain_grad, scale_grad):
    rows = query_grad.shape[0]
    query_grad[...] = found[0:rows]
    gain_grad[...] = found[rows : rows + 1]
    scale_grad[...] = found[rows + 1 : rows + 2]


def on_device(path_table, tokens, assign, out_grad, query_weights, gain, scale):
    n_dp = lax.axis_size("dp")
    n_sec = lax.axis_size("section")
    vocab, width = path_table.shape
    slots, seq = tokens.shape[1:]
    rows, hd = query_weights.shape[1:]
    count = slots * seq
    layers = n_sec
    plane, planes, heads = layout(n_dp, n_sec, width, hd)
    per_head = hd // rows
    pieces = heads * per_head
    n_dev = n_dp * n_sec
    held = heads * hd
    block_rows = plane * count // BLOCKS
    pairs = block_rows // (2 * seq)
    phases = max(1, 2 * layers - 2)
    first = lax.rem(lax.axis_index("dp") * rows, hd)
    if rows < hd:
        gain = lax.dynamic_update_slice(jnp.zeros((1, hd), BF16), gain, (0, first))
        scale = lax.dynamic_update_slice(jnp.zeros((1, hd), BF16), scale, (0, first))
    vmem = pl.BlockSpec(memory_space=pltpu.VMEM)
    hbm = pl.BlockSpec(memory_space=pl.ANY)
    stream = pltpu.VMEM((layers, BLOCKS, block_rows, held), BF16)
    found = pl.pallas_call(
        functools.partial(step_kernel, n_dp, n_sec),
        out_shape=pltpu.VMEM((rows + 8, hd), F32),
        in_specs=[hbm] * 7,
        out_specs=vmem,
        scratch_shapes=[
            pltpu.VMEM((slots, seq), jnp.int32),
            pltpu.SMEM((slots,), jnp.int32),
            pltpu.VMEM((1, hd), BF16),
            pltpu.VMEM((1, hd), BF16),
            pltpu.VMEM((rows + TAIL, hd), BF16),
            pltpu.VMEM((layers, pieces, rows + TAIL, hd), BF16),
            pltpu.VMEM((plane, 1, count), F32),
            pltpu.VMEM((vocab, width), BF16),
            pltpu.VMEM((vocab, held), BF16),
            pltpu.VMEM((block_rows, vocab), BF16),
            pltpu.VMEM((1, vocab), F32),
            pltpu.VMEM((BLOCKS, heads, block_rows, hd), BF16),
            stream,
            stream,
            stream,
            pltpu.VMEM((layers, BLOCKS, block_rows, held), F32),
            pltpu.VMEM((layers, BLOCKS, pairs, heads, seq, hd), F32),
            pltpu.VMEM((BLOCKS, block_rows, held), BF16),
            pltpu.VMEM((BLOCKS, block_rows, held), BF16),
            pltpu.VMEM((layers, BLOCKS, block_rows, hd), F32),
            pltpu.VMEM((layers, BLOCKS, 1, block_rows), F32),
            pltpu.VMEM((phases, BLOCKS, plane * n_sec, 1, block_rows), F32),
            pltpu.VMEM((heads, hd, hd), F32),
            pltpu.VMEM((8, held), F32),
            pltpu.VMEM((layers, pieces, rows, hd), BF16),
            pltpu.VMEM((planes, rows, hd), BF16),
            pltpu.VMEM((layers, pieces, TAIL, hd), BF16),
            pltpu.VMEM((planes, TAIL, hd), BF16),
            pltpu.VMEM((n_dev, 1, hd), F32),
            pltpu.SemaphoreType.DMA((5,)),
            pltpu.SemaphoreType.DMA,
            pltpu.SemaphoreType.DMA((heads,)),
            pltpu.SemaphoreType.DMA,
            pltpu.SemaphoreType.DMA,
            pltpu.SemaphoreType.DMA,
            pltpu.SemaphoreType.DMA((layers,)),
            pltpu.SemaphoreType.DMA,
            pltpu.SemaphoreType.DMA((BLOCKS,)),
            pltpu.SemaphoreType.DMA,
            pltpu.SemaphoreType.DMA((phases, BLOCKS)),
            pltpu.SemaphoreType.DMA,
            pltpu.SemaphoreType.DMA,
            pltpu.SemaphoreType.DMA,
            pltpu.SemaphoreType.DMA,
            pltpu.SemaphoreType.DMA,
            pltpu.SemaphoreType.DMA,
        ],
        compiler_params=pltpu.CompilerParams(
            collective_id=0, has_side_effects=True, vmem_limit_bytes=56 * 1024 * 1024
        ),
    )(
        path_table,
        tokens[0],
        assign[0],
        out_grad.reshape(count, width),
        query_weights[0],
        gain,
        scale,
    )
    query_grad, gain_grad, scale_grad = pl.pallas_call(
        split_kernel,
        out_shape=(
            jax.ShapeDtypeStruct((rows, hd), F32),
            jax.ShapeDtypeStruct((1, hd), F32),
            jax.ShapeDtypeStruct((1, hd), F32),
        ),
        in_specs=[vmem],
        out_specs=(vmem, vmem, vmem),
        compiler_params=pltpu.CompilerParams(vmem_limit_bytes=1024 * 1024),
    )(found)
    if rows < hd:
        gain_grad = lax.dynamic_slice(gain_grad, (0, first), (1, rows))
        scale_grad = lax.dynamic_slice(scale_grad, (0, first), (1, rows))
    return query_grad[None], gain_grad, scale_grad


def solution(mesh):
    in_specs = (
        P(),
        P("dp", None, None),
        P("dp", None),
        P("dp", None, None, None, None),
        P("section", "dp", None),
        P("section", "dp"),
        P("section", "dp"),
    )
    out_specs = (P("section", "dp", None), P("section", "dp"), P("section", "dp"))
    return jax.shard_map(
        on_device, mesh=mesh, in_specs=in_specs, out_specs=out_specs, check_vma=False
    )
```

```python
import functools
import math

import jax
import jax.numpy as jnp
from jax import lax
from jax.experimental import pallas as pl
from jax.experimental.pallas import tpu as pltpu
from jax.sharding import PartitionSpec as P

MESH = pl.DeviceIdType.MESH
F32 = jnp.float32
BF16 = jnp.bfloat16
TAIL = 16
PLANE = 4
BLOCKS = 2
SHARES = (2, 4, 6)
UNROLL = 32


def matmul(lhs, rhs, lhs_dim, rhs_dim):
    return lax.dot_general(
        lhs, rhs, (((lhs_dim,), (rhs_dim,)), ((), ())), preferred_element_type=F32
    )


def beside(parts, axis):
    return parts[0] if len(parts) == 1 else jnp.concatenate(parts, axis=axis)


def diagonal(parts):
    zero = jnp.zeros_like(parts[0])
    return beside(
        [
            beside([part if i == k else zero for k in range(len(parts))], 1)
            for i, part in enumerate(parts)
        ],
        0,
    )


def layout(n_dp, n_sec, width, hd):
    plane = math.gcd(n_dp, min(PLANE, width // hd // n_sec))
    return plane, n_dp // plane, width // hd // n_sec // plane


def step_kernel(
    n_dp,
    n_sec,
    table,
    tokens,
    assign,
    out_grad,
    weights,
    gain,
    scale,
    out,
    tokens_in,
    assign_in,
    gain_in,
    scale_in,
    packed,
    params,
    toks,
    tbl,
    emb,
    picked,
    table_rstd,
    cot,
    xs,
    normed,
    queries,
    mixed,
    probs,
    dnormed,
    dqueried,
    rstd,
    roots,
    parts,
    grads,
    tails,
    tx,
    rx,
    tail_tx,
    tail_rx,
    norms,
    in_sem,
    load_sem,
    emb_sem,
    t_send,
    t_recv,
    w_send,
    w_recv,
    c_send,
    c_recv,
    x_send,
    x_recv,
    g_send,
    g_recv,
    tg_send,
    tg_recv,
    n_send,
    n_recv,
):
    slots, seq = tokens.shape
    vocab, width = table.shape
    rows, hd = weights.shape
    plane, planes, heads = layout(n_dp, n_sec, width, hd)
    layers = n_sec
    per_head = hd // rows
    n_dev = n_dp * n_sec
    members = plane * n_sec
    held = heads * hd
    some = slots // BLOCKS * seq
    block_rows = plane * some
    two = 2 * seq
    pairs = block_rows // two
    inv = 1.0 / math.sqrt(hd)
    me_d = lax.axis_index("dp")
    me_s = lax.axis_index("section")
    me = me_d * n_sec + me_s
    me_z = lax.div(me_d, plane)
    me_p = lax.rem(me_d, plane)
    member = me_p * n_sec + me_s

    def repeat(first, last, body):
        if last - first <= UNROLL:
            for k in range(first, last):
                body(k)
        else:

            def step(k, carry):
                body(k)
                return carry

            lax.fori_loop(first, last, step, 0)

    def after(at, k, size):
        moved = at + k
        return jnp.where(moved >= size, moved - size, moved)

    def peers(size, at, body):
        if size * n_sec <= UNROLL:
            for kd in [*range(size // 2, size), *reversed(range(size // 2))]:
                d = after(at, kd, size) if kd else at
                for ks in range(n_sec):
                    if kd or ks:
                        body(d, after(me_s, ks, n_sec) if ks else me_s)
        else:

            def step(k, carry):
                t = lax.rem(at * n_sec + me_s + k, size * n_sec)
                body(lax.div(t, n_sec), lax.rem(t, n_sec))
                return carry

            lax.fori_loop(1, size * n_sec, step, 0)

    def head_of(p, c, hh):
        return (c * heads + hh) * plane + p

    def columns(h):
        return pl.ds(pl.multiple_of(h * hd, hd), hd)

    def lanes(hh):
        return slice(hh * hd, (hh + 1) * hd)

    def remote(src, dst, ssem, rsem, d, s):
        return pltpu.make_async_remote_copy(
            src_ref=src,
            dst_ref=dst,
            send_sem=ssem,
            recv_sem=rsem,
            device_id=(d, s),
            device_id_type=MESH,
        )

    barrier = pltpu.get_barrier_semaphore()

    def greet(d, s):
        pl.semaphore_signal(barrier, inc=1, device_id=(d, s), device_id_type=MESH)

    peers(n_dp, me_d, greet)
    pltpu.make_async_copy(table, tbl, load_sem).start()
    loads = [
        pltpu.make_async_copy(tokens, tokens_in, in_sem.at[0]),
        pltpu.make_async_copy(assign, assign_in, in_sem.at[1]),
        pltpu.make_async_copy(weights, packed.at[pl.ds(0, rows)], in_sem.at[2]),
        pltpu.make_async_copy(gain, gain_in, in_sem.at[3]),
        pltpu.make_async_copy(scale, scale_in, in_sem.at[4]),
    ]
    for load in loads:
        load.start()
    own_columns = [
        pltpu.make_async_copy(
            table.at[:, columns(head_of(me_p, me_s, hh))], emb.at[:, lanes(hh)], emb_sem.at[hh]
        )
        for hh in range(heads)
    ]
    for load in own_columns:
        load.start()

    def cot_at(blk, p, hh, start, size):
        return cot.at[blk, hh, pl.ds(p * some + start, size)]

    def cot_from(blk, h, start, size):
        return out_grad.at[pl.ds(blk * some + start, size), columns(h)]

    for blk in range(BLOCKS):
        for hh in range(heads):
            pltpu.make_async_copy(
                cot_from(blk, head_of(me_p, me_s, hh), 0, some),
                cot_at(blk, me_p, hh, 0, some),
                c_recv.at[blk],
            ).start()

    for load in loads:
        load.wait()
    tail_row = lax.broadcasted_iota(jnp.int32, (TAIL, hd), 0)
    packed[rows : rows + TAIL, :] = jnp.where(
        tail_row == 0,
        gain_in[...].astype(F32),
        jnp.where(tail_row == 1, scale_in[...].astype(F32), 0.0),
    ).astype(BF16)
    toks[me_p] = beside(
        [tokens_in[pl.ds(assign_in[j], 1), :].astype(F32) for j in range(slots)], 1
    )
    probs[...] = jnp.zeros(probs.shape, F32)

    pl.semaphore_wait(barrier, n_dev - 1)

    my_head = lax.div(me_d * rows, hd)
    to_p = lax.rem(my_head, plane)
    to_i = lax.div(my_head, plane)
    to_s = lax.div(to_i, heads)
    place = lax.rem(to_i, heads) * per_head + lax.rem(me_d, per_head)
    keep = (to_p == me_p) & (to_s == me_s)

    def give(k):
        z = lax.rem(me_z + k, planes)
        remote(
            packed, params.at[me_s, place], w_send, w_recv.at[me_s], z * plane + to_p, to_s
        ).start()

    def give_all():
        repeat(1, planes, give)

        @pl.when(keep)
        def _():
            pltpu.make_async_copy(packed, params.at[me_s, place], w_recv.at[me_s]).start()

        @pl.when(jnp.logical_not(keep))
        def _():
            remote(
                packed,
                params.at[me_s, place],
                w_send,
                w_recv.at[me_s],
                me_z * plane + to_p,
                to_s,
            ).start()

    pl.when(me_s == 0)(give_all)

    for k in range(1, plane):
        p = lax.rem(me_p + k, plane)
        remote(toks.at[me_p], toks.at[me_p], t_send, t_recv, me_z * plane + p, me_s).start()

    cuts = [sum(SHARES[:k]) * (some // 16) // sum(SHARES) * 16 for k in range(len(SHARES))]
    cuts.append(some)

    def send_cot(blk, begin, end):
        if begin == end:
            return
        for k in range(1, plane):
            p = lax.rem(me_p + k, plane)
            for hh in range(heads):
                remote(
                    cot_from(blk, head_of(p, me_s, hh), begin, end - begin),
                    cot_at(blk, me_p, hh, begin, end - begin),
                    c_send,
                    c_recv.at[blk],
                    me_z * plane + p,
                    me_s,
                ).start()

    for blk in range(BLOCKS - 1):
        send_cot(blk, 0, some)
    send_cot(BLOCKS - 1, cuts[0], cuts[1])

    ones_row = jnp.ones((TAIL, 2 * hd), BF16)
    ones_column = jnp.ones((TAIL, hd), BF16)

    def as_row(terms):
        high = terms.astype(BF16)
        low = (terms - high.astype(F32)).astype(BF16)
        return matmul(ones_row, beside([high, low], 1), 1, 1)[0:1]

    def as_column(row):
        at = lax.broadcasted_iota(jnp.int32, (TAIL, row.shape[1]), 0)
        high = row.astype(BF16).astype(F32)
        mid = (row - high).astype(BF16).astype(F32)
        low = row - high - mid
        stack = jnp.where(at == 0, high, jnp.where(at == 1, mid, jnp.where(at == 2, low, 0.0)))
        return matmul(stack.astype(BF16), ones_column, 0, 0)

    def exchange(phase, blk, terms):
        parts[phase, blk, member] = as_row(terms)

        def share(p, s):
            remote(
                parts.at[phase, blk, member],
                parts.at[phase, blk, member],
                x_send,
                x_recv.at[phase, blk],
                me_z * plane + p,
                s,
            ).start()

        peers(plane, me_p, share)

    def exchanged(phase, blk):
        if members > 1:
            whole = parts.at[phase, blk, pl.ds(0, members - 1)]
            pltpu.make_async_copy(whole, whole, x_recv.at[phase, blk]).wait()
        return jnp.sum(parts[phase, blk], axis=0)

    def layer_param(b, hh):
        at = hh * per_head
        tail = params[b, at, rows:, :].astype(F32)
        weight = params[b, at, :rows, :]
        if per_head > 1:
            for i in range(1, per_head):
                tail = tail + params[b, at + i, rows:, :].astype(F32)
            weight = jnp.concatenate(
                [params[b, at + i, :rows, :] for i in range(per_head)], axis=0
            )
        return weight, tail[0:1], tail[1:2]

    def layer_params(b):
        found = [layer_param(b, hh) for hh in range(heads)]
        return (
            diagonal([one[0] for one in found]),
            beside([one[1] for one in found], 1),
            beside([one[2] for one in found], 1),
        )

    at_row = lax.broadcasted_iota(jnp.int32, (seq, two), 0)
    at_col = lax.broadcasted_iota(jnp.int32, (seq, two), 1)
    first = at_col < seq
    allowed = at_row <= jnp.where(first, at_col, at_col - seq)
    wide_col = lax.broadcasted_iota(jnp.int32, (seq, hd), 1)
    wide_first = wide_col < seq
    wide_second = (wide_col >= seq) & (wide_col < two)
    vocab_lane = lax.broadcasted_iota(jnp.int32, (some, hd), 1).astype(F32)

    def wide(column):
        return beside([column] * heads, 1)

    def both(sides):
        return sides[:, :hd] if heads == 1 else sum(sides[:, lanes(hh)] for hh in range(heads))

    def embed(blk):
        for p in range(plane):
            col = as_column(toks[p, :, blk * some : (blk + 1) * some])
            at = slice(p * some, (p + 1) * some)
            root = jnp.zeros((some, hd), F32)
            for v in range(vocab // hd):
                hit = vocab_lane + float(v * hd) == col
                picked[at, lanes(v)] = jnp.where(hit, 1.0, 0.0).astype(BF16)
                root = root + jnp.where(hit, table_rstd[:, lanes(v)], 0.0)
            rstd[0, blk, at] = jnp.broadcast_to(jnp.sum(root, axis=1, keepdims=True), (some, hd))
        xs[0, blk] = matmul(picked[...], emb[...], 1, 0).astype(BF16)

    def forward(b, blk):
        if b > 0:
            root = lax.rsqrt(exchanged(b - 1, blk) * (1.0 / width) + 1e-05)
            roots[b, blk] = root
            rstd[b, blk] = as_column(root)
        weight, gain_row, scale_row = layer_params(b)
        norm = (xs[b, blk].astype(F32) * wide(rstd[b, blk]) * gain_row).astype(BF16)
        normed[b, blk] = norm
        query = (matmul(norm, weight, 1, 0) * inv).astype(BF16)
        queries[b, blk] = query
        tiles = [(p, hh) for p in range(pairs) for hh in range(heads)]
        scores = []
        for p, hh in tiles:
            lo, mid, hi = p * two, p * two + seq, (p + 1) * two
            scores.append(
                matmul(
                    beside([norm[lo:mid, lanes(hh)], norm[mid:hi, lanes(hh)]], 1),
                    diagonal([query[lo:mid, lanes(hh)], query[mid:hi, lanes(hh)]]),
                    1,
                    1,
                )
            )
        spread = {}
        for (p, hh), score in zip(tiles, scores):
            score = jnp.where(allowed, score, -1e30)
            raised = jnp.exp(score - jnp.max(score, axis=0, keepdims=True))
            attend = raised * (1.0 / jnp.sum(raised, axis=0, keepdims=True))
            probs[b, blk, p, hh, :, 0:two] = attend
            if b + 1 < layers:
                spread[p, hh] = spread_out(attend)
        if b + 1 == layers:
            return
        terms = []
        for p in range(pairs):
            lo, hi = p * two, (p + 1) * two
            mix = mixed_rows(norm, spread, p)
            mixed[b, blk, lo:hi] = mix
            out_rows = (xs[b, blk, lo:hi].astype(F32) + scale_row * mix).astype(BF16)
            xs[b + 1, blk, lo:hi] = out_rows
            out_rows = out_rows.astype(F32)
            terms.append(both(out_rows * out_rows))
        exchange(b, blk, beside(terms, 0))

    def spread_out(attend):
        attend = attend.astype(BF16)
        zero = jnp.zeros_like(attend)
        return [jnp.where(first, attend, zero), jnp.where(first, zero, attend)]

    def mixed_rows(norm, spread, p):
        lo, hi = p * two, (p + 1) * two
        return matmul(
            beside([part for hh in range(heads) for part in spread[p, hh]], 0),
            diagonal([norm[lo:hi, lanes(hh)] for hh in range(heads)]),
            0,
            0,
        )

    def backward(b, blk):
        if b + 1 == layers:
            pltpu.make_async_copy(cot.at[blk], cot.at[blk], c_recv.at[blk]).wait()
        else:
            inner = exchanged(layers - 1 + b, blk) * (1.0 / width)
            root = roots[b + 1, blk]
            along = as_column(inner * root * root * root)
            _, gain_row, _ = layer_params(b + 1)
            dy = dnormed[blk].astype(F32) * gain_row
            back = wide(rstd[b + 1, blk]) * dy - xs[b + 1, blk].astype(F32) * wide(along)
        weight, gain_row, scale_row = layer_params(b)
        given = beside([cot[blk, hh] for hh in range(heads)], 1).astype(F32)
        if b + 1 < layers:
            given = (given + back).astype(BF16)
            if b > 0:
                for hh in range(heads):
                    cot[blk, hh] = given[:, lanes(hh)]
            given = given.astype(F32)
            add_tail(1, blk, jnp.sum(given * mixed[b, blk], axis=0, keepdims=True))
        dmix = (given * scale_row).astype(BF16)
        tiles = [(p, hh) for p in range(pairs) for hh in range(heads)]
        gap = jnp.zeros((hd - two, hd), BF16)
        wide_gap = jnp.zeros((hd - two, 2 * hd), BF16)
        datts = []
        for p, hh in tiles:
            lo, mid, hi = p * two, p * two + seq, (p + 1) * two
            datts.append(
                matmul(
                    beside(
                        [normed[b, blk, lo:mid, lanes(hh)], normed[b, blk, mid:hi, lanes(hh)]], 1
                    ),
                    beside(
                        [diagonal([dmix[lo:mid, lanes(hh)], dmix[mid:hi, lanes(hh)]]), wide_gap],
                        0,
                    ),
                    1,
                    1,
                )
            )
        dscores, attends = {}, {}
        for (p, hh), datt in zip(tiles, datts):
            datt = datt.astype(BF16).astype(F32)
            attend = probs[b, blk, p, hh]
            inner = jnp.sum(datt * attend, axis=0, keepdims=True)
            dscore = (attend * (datt - inner)).astype(BF16)
            attend = attend.astype(BF16)
            zero = jnp.zeros_like(dscore)
            dscores[p, hh] = beside(
                [jnp.where(wide_first, dscore, zero), jnp.where(wide_second, dscore, zero)], 0
            )
            attends[p, hh] = beside(
                [jnp.where(wide_first, attend, zero), jnp.where(wide_second, attend, zero)], 0
            )
        dqueries, dnorms = [], []
        for p in range(pairs):
            lo, hi = p * two, (p + 1) * two
            dquery = matmul(
                beside([dscores[p, hh] for hh in range(heads)], 0),
                diagonal([normed[b, blk, lo:hi, lanes(hh)] for hh in range(heads)]),
                0,
                0,
            )
            dqueries.append(dquery[:two].astype(BF16))
            dnorms.append(
                beside(
                    [
                        matmul(
                            beside([dscores[p, hh], attends[p, hh]], 1),
                            beside(
                                [
                                    queries[b, blk, lo:hi, lanes(hh)],
                                    gap,
                                    dmix[lo:hi, lanes(hh)],
                                    gap,
                                ],
                                0,
                            ),
                            1,
                            0,
                        )
                        for hh in range(heads)
                    ],
                    1,
                )
            )
        dquery = beside(dqueries, 0)

        if b == 0:
            for hh in range(heads):
                grad = matmul(normed[b, blk, :, lanes(hh)], dquery[:, lanes(hh)], 0, 0)
                if blk > 0:
                    grad = grad + grads[hh]
                grads[hh] = grad
            if blk + 1 == BLOCKS:
                send_grads(b)
        else:
            dqueried[blk] = dquery
        dnorm = beside(dnorms, 0) + matmul(dquery, weight, 1, 1) * inv
        dnorm = dnorm.astype(BF16)
        if b > 0:
            dnormed[blk] = dnorm
            x_in = xs[b, blk].astype(F32)
            exchange(layers - 2 + b, blk, both(dnorm.astype(F32) * gain_row * x_in))
        else:
            add_gain(b, blk, dnorm)
            if blk + 1 == BLOCKS:
                send_tails(b)

    def add_tail(row, blk, part):
        if blk > 0:
            part = part + tails[row : row + 1]
        tails[row : row + 1] = part

    def add_gain(b, blk, dnorm):
        unit = xs[b, blk].astype(F32) * wide(rstd[b, blk])
        add_tail(0, blk, jnp.sum(dnorm.astype(F32) * unit, axis=0, keepdims=True))

    def later_grads(b):
        for hh in range(heads):
            grads[hh] = matmul(
                beside([normed[b, blk, :, lanes(hh)] for blk in range(BLOCKS)], 0),
                beside([dqueried[blk, :, lanes(hh)] for blk in range(BLOCKS)], 0),
                0,
                0,
            )
        send_grads(b)

    def later_tails(b):
        for blk in range(BLOCKS):
            add_gain(b, blk, dnormed[blk])
            if b + 1 < layers:
                continue
            norm = normed[b, blk]
            spread = {
                (p, hh): spread_out(probs[b, blk, p, hh, :, 0:two])
                for p in range(pairs)
                for hh in range(heads)
            }
            mix = beside([mixed_rows(norm, spread, p) for p in range(pairs)], 0)
            given = beside([cot[blk, hh] for hh in range(heads)], 1).astype(F32)
            add_tail(1, blk, jnp.sum(given * mix, axis=0, keepdims=True))
        send_tails(b)

    def give_grads(b, source, target, sent, arrived):
        for hh in range(heads):
            for i in range(per_head):
                at = hh * per_head + i
                r = head_of(me_p, me_s, hh) * per_head + i
                mine = (r == me_d) & (me_s == b)

                @pl.when(mine)
                def _():
                    pltpu.make_async_copy(source.at[b, at], target.at[me_z], arrived).start()

                @pl.when(jnp.logical_not(mine))
                def _():
                    remote(source.at[b, at], target.at[me_z], sent, arrived, r, b).start()

    def send_grads(b):
        for hh in range(heads):
            dweight = (grads[hh] * inv).astype(BF16)
            for i in range(per_head):
                tx[b, hh * per_head + i] = dweight[i * rows : (i + 1) * rows]
        give_grads(b, tx, rx, g_send, g_recv)

    def send_tails(b):
        for hh in range(heads):
            gain_part, scale_part = tails[0:1, lanes(hh)], tails[1:2, lanes(hh)]
            gain_hi = gain_part.astype(BF16).astype(F32)
            scale_hi = scale_part.astype(BF16).astype(F32)
            tail = jnp.where(
                tail_row == 0,
                gain_hi,
                jnp.where(
                    tail_row == 1,
                    gain_part - gain_hi,
                    jnp.where(
                        tail_row == 2,
                        scale_hi,
                        jnp.where(tail_row == 3, scale_part - scale_hi, 0.0),
                    ),
                ),
            ).astype(BF16)
            for i in range(per_head):
                tail_tx[b, hh * per_head + i] = tail
        give_grads(b, tail_tx, tail_rx, tg_send, tg_recv)

    pltpu.make_async_copy(tbl, tbl, load_sem).wait()
    chunk = math.gcd(vocab, 128)

    def table_norm(i, carry):
        at = pl.ds(pl.multiple_of(i * chunk, chunk), chunk)
        squares = jnp.zeros((chunk, hd), F32)
        for h in range(width // hd):
            block = tbl[at, h * hd : (h + 1) * hd].astype(F32)
            squares = squares + block * block
        table_rstd[:, at] = lax.rsqrt(as_row(squares) * (1.0 / width) + 1e-05)
        return carry

    lax.fori_loop(0, vocab // chunk, table_norm, 0)

    for load in own_columns:
        load.wait()
    if plane > 1:
        pltpu.make_async_copy(
            toks.at[pl.ds(0, plane - 1)], toks.at[pl.ds(0, plane - 1)], t_recv
        ).wait()
    embed(0)
    pl.when(me_s > 0)(give_all)
    for b in range(layers):
        pltpu.make_async_copy(params.at[b], params.at[b], w_recv.at[b]).wait()
        for blk in range(BLOCKS):
            if b == 0 and blk > 0:
                embed(blk)
            forward(b, blk)
            if b == 0:
                send_cot(BLOCKS - 1, cuts[blk + 1], cuts[blk + 2])
            if b + 1 == layers:
                backward(b, blk)
    for b in reversed(range(layers - 1)):
        later_grads(b + 1)
        later_tails(b + 1)
        for blk in range(BLOCKS):
            backward(b, blk)

    pltpu.make_async_copy(rx, rx, g_recv).wait()
    total_query = jnp.sum(rx[...].astype(F32), axis=0)
    query_squares = jnp.sum(total_query * total_query, axis=0, keepdims=True)
    pltpu.make_async_copy(tail_rx, tail_rx, tg_recv).wait()
    total = jnp.sum(tail_rx[...].astype(F32), axis=0)
    total_gain = total[0:1] + total[1:2]
    total_scale = total[2:3] + total[3:4]
    if per_head > 1:
        at = lax.broadcasted_iota(jnp.int32, (1, hd), 1)
        start = lax.rem(me_d, per_head) * rows
        inside = (at >= start) & (at < start + rows)
        total_gain = jnp.where(inside, total_gain, 0.0)
        total_scale = jnp.where(inside, total_scale, 0.0)
    squares = (
        query_squares
        + total_gain * total_gain
        + total_scale * total_scale
    )
    norms[pl.ds(me, 1)] = squares[None]

    def tell(d, s):
        remote(norms.at[me], norms.at[me], n_send, n_recv, d, s).start()

    peers(n_dp, me_d, tell)

    if members > 1:
        for phase in range(2 * layers - 2):
            whole = parts.at[phase, :, pl.ds(0, members - 1)]
            pltpu.make_async_copy(whole, whole, x_send).wait()
    if plane > 1:
        sent = toks.at[pl.ds(0, plane - 1)]
        pltpu.make_async_copy(sent, sent, t_send).wait()
        sent = cot.at[:, :, pl.ds(0, (plane - 1) * some)]
        pltpu.make_async_copy(sent, sent, c_send).wait()

    def sent_weight(k, carry):
        pltpu.make_async_copy(packed, packed, w_send).wait()
        return carry

    lax.fori_loop(0, jnp.where(keep, planes - 1, planes), sent_weight, 0)

    def sent_grad(k, carry):
        pltpu.make_async_copy(rx.at[0], rx.at[0], g_send).wait()
        pltpu.make_async_copy(tail_rx.at[0], tail_rx.at[0], tg_send).wait()
        return carry

    pieces = layers * heads * per_head
    lax.fori_loop(0, jnp.where(keep, pieces - 1, pieces), sent_grad, 0)

    others = norms.at[pl.ds(0, n_dev - 1)]
    pltpu.make_async_copy(others, others, n_recv).wait()
    overall = jnp.sum(jnp.sum(norms[...], axis=0), axis=1, keepdims=True)
    limit = float(layers * width * (hd + 2))
    factor = jnp.minimum(1.0, math.sqrt(limit) / jnp.sqrt(overall))
    out[0:rows] = total_query * factor
    out[rows : rows + 8] = jnp.where(
        lax.broadcasted_iota(jnp.int32, (8, hd), 0) == 0, total_gain * factor, total_scale * factor
    )
    pltpu.make_async_copy(others, others, n_send).wait()


def split_kernel(found, query_grad, gain_grad, scale_grad):
    rows = query_grad.shape[0]
    query_grad[...] = found[0:rows]
    gain_grad[...] = found[rows : rows + 1]
    scale_grad[...] = found[rows + 1 : rows + 2]


def on_device(path_table, tokens, assign, out_grad, query_weights, gain, scale):
    n_dp = lax.axis_size("dp")
    n_sec = lax.axis_size("section")
    vocab, width = path_table.shape
    slots, seq = tokens.shape[1:]
    rows, hd = query_weights.shape[1:]
    count = slots * seq
    layers = n_sec
    plane, planes, heads = layout(n_dp, n_sec, width, hd)
    per_head = hd // rows
    pieces = heads * per_head
    n_dev = n_dp * n_sec
    held = heads * hd
    block_rows = plane * count // BLOCKS
    pairs = block_rows // (2 * seq)
    phases = max(1, 2 * layers - 2)
    first = lax.rem(lax.axis_index("dp") * rows, hd)
    if rows < hd:
        gain = lax.dynamic_update_slice(jnp.zeros((1, hd), BF16), gain, (0, first))
        scale = lax.dynamic_update_slice(jnp.zeros((1, hd), BF16), scale, (0, first))
    vmem = pl.BlockSpec(memory_space=pltpu.VMEM)
    hbm = pl.BlockSpec(memory_space=pl.ANY)
    stream = pltpu.VMEM((layers, BLOCKS, block_rows, held), BF16)
    found = pl.pallas_call(
        functools.partial(step_kernel, n_dp, n_sec),
        out_shape=pltpu.VMEM((rows + 8, hd), F32),
        in_specs=[hbm] * 7,
        out_specs=vmem,
        scratch_shapes=[
            pltpu.VMEM((slots, seq), jnp.int32),
            pltpu.SMEM((slots,), jnp.int32),
            pltpu.VMEM((1, hd), BF16),
            pltpu.VMEM((1, hd), BF16),
            pltpu.VMEM((rows + TAIL, hd), BF16),
            pltpu.VMEM((layers, pieces, rows + TAIL, hd), BF16),
            pltpu.VMEM((plane, 1, count), F32),
            pltpu.VMEM((vocab, width), BF16),
            pltpu.VMEM((vocab, held), BF16),
            pltpu.VMEM((block_rows, vocab), BF16),
            pltpu.VMEM((1, vocab), F32),
            pltpu.VMEM((BLOCKS, heads, block_rows, hd), BF16),
            stream,
            stream,
            stream,
            pltpu.VMEM((layers, BLOCKS, block_rows, held), F32),
            pltpu.VMEM((layers, BLOCKS, pairs, heads, seq, hd), F32),
            pltpu.VMEM((BLOCKS, block_rows, held), BF16),
            pltpu.VMEM((BLOCKS, block_rows, held), BF16),
            pltpu.VMEM((layers, BLOCKS, block_rows, hd), F32),
            pltpu.VMEM((layers, BLOCKS, 1, block_rows), F32),
            pltpu.VMEM((phases, BLOCKS, plane * n_sec, 1, block_rows), F32),
            pltpu.VMEM((heads, hd, hd), F32),
            pltpu.VMEM((8, held), F32),
            pltpu.VMEM((layers, pieces, rows, hd), BF16),
            pltpu.VMEM((planes, rows, hd), BF16),
            pltpu.VMEM((layers, pieces, TAIL, hd), BF16),
            pltpu.VMEM((planes, TAIL, hd), BF16),
            pltpu.VMEM((n_dev, 1, hd), F32),
            pltpu.SemaphoreType.DMA((5,)),
            pltpu.SemaphoreType.DMA,
            pltpu.SemaphoreType.DMA((heads,)),
            pltpu.SemaphoreType.DMA,
            pltpu.SemaphoreType.DMA,
            pltpu.SemaphoreType.DMA,
            pltpu.SemaphoreType.DMA((layers,)),
            pltpu.SemaphoreType.DMA,
            pltpu.SemaphoreType.DMA((BLOCKS,)),
            pltpu.SemaphoreType.DMA,
            pltpu.SemaphoreType.DMA((phases, BLOCKS)),
            pltpu.SemaphoreType.DMA,
            pltpu.SemaphoreType.DMA,
            pltpu.SemaphoreType.DMA,
            pltpu.SemaphoreType.DMA,
            pltpu.SemaphoreType.DMA,
            pltpu.SemaphoreType.DMA,
        ],
        compiler_params=pltpu.CompilerParams(
            collective_id=0, has_side_effects=True, vmem_limit_bytes=56 * 1024 * 1024
        ),
    )(
        path_table,
        tokens[0],
        assign[0],
        out_grad.reshape(count, width),
        query_weights[0],
        gain,
        scale,
    )
    query_grad, gain_grad, scale_grad = pl.pallas_call(
        split_kernel,
        out_shape=(
            jax.ShapeDtypeStruct((rows, hd), F32),
            jax.ShapeDtypeStruct((1, hd), F32),
            jax.ShapeDtypeStruct((1, hd), F32),
        ),
        in_specs=[vmem],
        out_specs=(vmem, vmem, vmem),
        compiler_params=pltpu.CompilerParams(vmem_limit_bytes=1024 * 1024),
    )(found)
    if rows < hd:
        gain_grad = lax.dynamic_slice(gain_grad, (0, first), (1, rows))
        scale_grad = lax.dynamic_slice(scale_grad, (0, first), (1, rows))
    return query_grad[None], gain_grad, scale_grad


def solution(mesh):
    in_specs = (
        P(),
        P("dp", None, None),
        P("dp", None),
        P("dp", None, None, None, None),
        P("section", "dp", None),
        P("section", "dp"),
        P("section", "dp"),
    )
    out_specs = (P("section", "dp", None), P("section", "dp"), P("section", "dp"))
    return jax.shard_map(
        on_device, mesh=mesh, in_specs=in_specs, out_specs=out_specs, check_vma=False
    )
```

```python
import functools
import math

import jax
import jax.numpy as jnp
from jax import lax
from jax.experimental import pallas as pl
from jax.experimental.pallas import tpu as pltpu
from jax.sharding import PartitionSpec as P

MESH = pl.DeviceIdType.MESH
F32 = jnp.float32
BF16 = jnp.bfloat16
TAIL = 16
PLANE = 4
BLOCKS = 2
SHARES = (2, 4, 6)
UNROLL = 32


def matmul(lhs, rhs, lhs_dim, rhs_dim):
    return lax.dot_general(
        lhs, rhs, (((lhs_dim,), (rhs_dim,)), ((), ())), preferred_element_type=F32
    )


def beside(parts, axis):
    return parts[0] if len(parts) == 1 else jnp.concatenate(parts, axis=axis)


def diagonal(parts):
    zero = jnp.zeros_like(parts[0])
    return beside(
        [
            beside([part if i == k else zero for k in range(len(parts))], 1)
            for i, part in enumerate(parts)
        ],
        0,
    )


def layout(n_dp, n_sec, width, hd):
    plane = math.gcd(n_dp, min(PLANE, width // hd // n_sec))
    return plane, n_dp // plane, width // hd // n_sec // plane


def step_kernel(
    n_dp,
    n_sec,
    table,
    tokens,
    assign,
    out_grad,
    weights,
    gain,
    scale,
    out,
    tokens_in,
    assign_in,
    gain_in,
    scale_in,
    packed,
    params,
    toks,
    tbl,
    emb,
    picked,
    table_rstd,
    cot,
    xs,
    normed,
    queries,
    mixed,
    probs,
    dnormed,
    dqueried,
    rstd,
    roots,
    parts,
    grads,
    tails,
    tx,
    rx,
    tail_tx,
    tail_rx,
    norms,
    in_sem,
    load_sem,
    emb_sem,
    t_send,
    t_recv,
    w_send,
    w_recv,
    c_send,
    c_recv,
    x_send,
    x_recv,
    g_send,
    g_recv,
    tg_send,
    tg_recv,
    n_send,
    n_recv,
):
    slots, seq = tokens.shape
    vocab, width = table.shape
    rows, hd = weights.shape
    plane, planes, heads = layout(n_dp, n_sec, width, hd)
    layers = n_sec
    per_head = hd // rows
    n_dev = n_dp * n_sec
    members = plane * n_sec
    held = heads * hd
    some = slots // BLOCKS * seq
    block_rows = plane * some
    two = 2 * seq
    pairs = block_rows // two
    inv = 1.0 / math.sqrt(hd)
    me_d = lax.axis_index("dp")
    me_s = lax.axis_index("section")
    me = me_d * n_sec + me_s
    me_z = lax.div(me_d, plane)
    me_p = lax.rem(me_d, plane)
    member = me_p * n_sec + me_s

    def repeat(first, last, body):
        if last - first <= UNROLL:
            for k in range(first, last):
                body(k)
        else:

            def step(k, carry):
                body(k)
                return carry

            lax.fori_loop(first, last, step, 0)

    def after(at, k, size):
        moved = at + k
        return jnp.where(moved >= size, moved - size, moved)

    def peers(size, at, body):
        if size * n_sec <= UNROLL:
            for kd in [*range(size // 2, size), *reversed(range(size // 2))]:
                d = after(at, kd, size) if kd else at
                for ks in range(n_sec):
                    if kd or ks:
                        body(d, after(me_s, ks, n_sec) if ks else me_s)
        else:

            def step(k, carry):
                t = lax.rem(at * n_sec + me_s + k, size * n_sec)
                body(lax.div(t, n_sec), lax.rem(t, n_sec))
                return carry

            lax.fori_loop(1, size * n_sec, step, 0)

    def head_of(p, c, hh):
        return (c * heads + hh) * plane + p

    def columns(h):
        return pl.ds(pl.multiple_of(h * hd, hd), hd)

    def lanes(hh):
        return slice(hh * hd, (hh + 1) * hd)

    def remote(src, dst, ssem, rsem, d, s):
        return pltpu.make_async_remote_copy(
            src_ref=src,
            dst_ref=dst,
            send_sem=ssem,
            recv_sem=rsem,
            device_id=(d, s),
            device_id_type=MESH,
        )

    barrier = pltpu.get_barrier_semaphore()

    def greet(d, s):
        pl.semaphore_signal(barrier, inc=1, device_id=(d, s), device_id_type=MESH)

    peers(n_dp, me_d, greet)
    pltpu.make_async_copy(table, tbl, load_sem).start()
    loads = [
        pltpu.make_async_copy(tokens, tokens_in, in_sem.at[0]),
        pltpu.make_async_copy(assign, assign_in, in_sem.at[1]),
        pltpu.make_async_copy(weights, packed.at[pl.ds(0, rows)], in_sem.at[2]),
        pltpu.make_async_copy(gain, gain_in, in_sem.at[3]),
        pltpu.make_async_copy(scale, scale_in, in_sem.at[4]),
    ]
    for load in loads:
        load.start()
    own_columns = [
        pltpu.make_async_copy(
            table.at[:, columns(head_of(me_p, me_s, hh))], emb.at[:, lanes(hh)], emb_sem.at[hh]
        )
        for hh in range(heads)
    ]
    for load in own_columns:
        load.start()

    def cot_at(blk, p, hh, start, size):
        return cot.at[blk, hh, pl.ds(p * some + start, size)]

    def cot_from(blk, h, start, size):
        return out_grad.at[pl.ds(blk * some + start, size), columns(h)]

    for blk in range(BLOCKS):
        for hh in range(heads):
            pltpu.make_async_copy(
                cot_from(blk, head_of(me_p, me_s, hh), 0, some),
                cot_at(blk, me_p, hh, 0, some),
                c_recv.at[blk],
            ).start()

    for load in loads:
        load.wait()
    tail_row = lax.broadcasted_iota(jnp.int32, (TAIL, hd), 0)
    packed[rows : rows + TAIL, :] = jnp.where(
        tail_row == 0,
        gain_in[...].astype(F32),
        jnp.where(tail_row == 1, scale_in[...].astype(F32), 0.0),
    ).astype(BF16)
    toks[me_p] = beside(
        [tokens_in[pl.ds(assign_in[j], 1), :].astype(F32) for j in range(slots)], 1
    )

    pl.semaphore_wait(barrier, n_dev - 1)

    my_head = lax.div(me_d * rows, hd)
    to_p = lax.rem(my_head, plane)
    to_i = lax.div(my_head, plane)
    to_s = lax.div(to_i, heads)
    place = lax.rem(to_i, heads) * per_head + lax.rem(me_d, per_head)
    keep = (to_p == me_p) & (to_s == me_s)

    def give(k):
        z = lax.rem(me_z + k, planes)
        remote(
            packed, params.at[me_s, place], w_send, w_recv.at[me_s], z * plane + to_p, to_s
        ).start()

    def give_all():
        repeat(1, planes, give)

        @pl.when(keep)
        def _():
            pltpu.make_async_copy(packed, params.at[me_s, place], w_recv.at[me_s]).start()

        @pl.when(jnp.logical_not(keep))
        def _():
            remote(
                packed,
                params.at[me_s, place],
                w_send,
                w_recv.at[me_s],
                me_z * plane + to_p,
                to_s,
            ).start()

    pl.when(me_s == 0)(give_all)

    for k in range(1, plane):
        p = lax.rem(me_p + k, plane)
        remote(toks.at[me_p], toks.at[me_p], t_send, t_recv, me_z * plane + p, me_s).start()

    cuts = [sum(SHARES[:k]) * (some // 16) // sum(SHARES) * 16 for k in range(len(SHARES))]
    cuts.append(some)

    def send_cot(blk, begin, end):
        if begin == end:
            return
        for k in range(1, plane):
            p = lax.rem(me_p + k, plane)
            for hh in range(heads):
                remote(
                    cot_from(blk, head_of(p, me_s, hh), begin, end - begin),
                    cot_at(blk, me_p, hh, begin, end - begin),
                    c_send,
                    c_recv.at[blk],
                    me_z * plane + p,
                    me_s,
                ).start()

    for blk in range(BLOCKS - 1):
        send_cot(blk, 0, some)
    send_cot(BLOCKS - 1, cuts[0], cuts[1])

    ones_row = jnp.ones((TAIL, 2 * hd), BF16)
    ones_column = jnp.ones((TAIL, hd), BF16)

    def as_row(terms):
        high = terms.astype(BF16)
        low = (terms - high.astype(F32)).astype(BF16)
        return matmul(ones_row, beside([high, low], 1), 1, 1)[0:1]

    def as_column(row):
        at = lax.broadcasted_iota(jnp.int32, (TAIL, row.shape[1]), 0)
        high = row.astype(BF16).astype(F32)
        mid = (row - high).astype(BF16).astype(F32)
        low = row - high - mid
        stack = jnp.where(at == 0, high, jnp.where(at == 1, mid, jnp.where(at == 2, low, 0.0)))
        return matmul(stack.astype(BF16), ones_column, 0, 0)

    def exchange(phase, blk, terms):
        parts[phase, blk, member] = as_row(terms)

        def share(p, s):
            remote(
                parts.at[phase, blk, member],
                parts.at[phase, blk, member],
                x_send,
                x_recv.at[phase, blk],
                me_z * plane + p,
                s,
            ).start()

        peers(plane, me_p, share)

    def exchanged(phase, blk):
        if members > 1:
            whole = parts.at[phase, blk, pl.ds(0, members - 1)]
            pltpu.make_async_copy(whole, whole, x_recv.at[phase, blk]).wait()
        return jnp.sum(parts[phase, blk], axis=0)

    def layer_param(b, hh):
        at = hh * per_head
        tail = params[b, at, rows:, :].astype(F32)
        weight = params[b, at, :rows, :]
        if per_head > 1:
            for i in range(1, per_head):
                tail = tail + params[b, at + i, rows:, :].astype(F32)
            weight = jnp.concatenate(
                [params[b, at + i, :rows, :] for i in range(per_head)], axis=0
            )
        return weight, tail[0:1], tail[1:2]

    def layer_params(b):
        found = [layer_param(b, hh) for hh in range(heads)]
        return (
            diagonal([one[0] for one in found]),
            beside([one[1] for one in found], 1),
            beside([one[2] for one in found], 1),
        )

    at_row = lax.broadcasted_iota(jnp.int32, (seq, two), 0)
    at_col = lax.broadcasted_iota(jnp.int32, (seq, two), 1)
    first = at_col < seq
    allowed = at_row <= jnp.where(first, at_col, at_col - seq)
    vocab_lane = lax.broadcasted_iota(jnp.int32, (some, hd), 1).astype(F32)

    def wide(column):
        return beside([column] * heads, 1)

    def both(sides):
        return sides[:, :hd] if heads == 1 else sum(sides[:, lanes(hh)] for hh in range(heads))

    def embed(blk):
        for p in range(plane):
            col = as_column(toks[p, :, blk * some : (blk + 1) * some])
            at = slice(p * some, (p + 1) * some)
            root = jnp.zeros((some, hd), F32)
            for v in range(vocab // hd):
                hit = vocab_lane + float(v * hd) == col
                picked[at, lanes(v)] = jnp.where(hit, 1.0, 0.0).astype(BF16)
                root = root + jnp.where(hit, table_rstd[:, lanes(v)], 0.0)
            rstd[0, blk, at] = jnp.broadcast_to(jnp.sum(root, axis=1, keepdims=True), (some, hd))
        xs[0, blk] = matmul(picked[...], emb[...], 1, 0).astype(BF16)

    def forward(b, blk):
        if b > 0:
            root = lax.rsqrt(exchanged(b - 1, blk) * (1.0 / width) + 1e-05)
            roots[b, blk] = root
            rstd[b, blk] = as_column(root)
        weight, gain_row, scale_row = layer_params(b)
        norm = (xs[b, blk].astype(F32) * wide(rstd[b, blk]) * gain_row).astype(BF16)
        normed[b, blk] = norm
        query = (matmul(norm, weight, 1, 0) * inv).astype(BF16)
        queries[b, blk] = query
        tiles = [(p, hh) for p in range(pairs) for hh in range(heads)]
        scores = []
        for p, hh in tiles:
            lo, mid, hi = p * two, p * two + seq, (p + 1) * two
            scores.append(
                matmul(
                    beside([norm[lo:mid, lanes(hh)], norm[mid:hi, lanes(hh)]], 1),
                    diagonal([query[lo:mid, lanes(hh)], query[mid:hi, lanes(hh)]]),
                    1,
                    1,
                )
            )
        spread = {}
        for (p, hh), score in zip(tiles, scores):
            score = jnp.where(allowed, score, -1e30)
            raised = jnp.exp(score - jnp.max(score, axis=0, keepdims=True))
            attend = raised * (1.0 / jnp.sum(raised, axis=0, keepdims=True))
            probs[b, blk, p, hh] = attend
            if b + 1 < layers:
                spread[p, hh] = spread_out(attend)
        if b + 1 == layers:
            return
        terms = []
        for p in range(pairs):
            lo, hi = p * two, (p + 1) * two
            mix = mixed_rows(norm, spread, p)
            mixed[b, blk, lo:hi] = mix
            out_rows = (xs[b, blk, lo:hi].astype(F32) + scale_row * mix).astype(BF16)
            xs[b + 1, blk, lo:hi] = out_rows
            out_rows = out_rows.astype(F32)
            terms.append(both(out_rows * out_rows))
        exchange(b, blk, beside(terms, 0))

    def spread_out(attend):
        attend = attend.astype(BF16)
        zero = jnp.zeros_like(attend)
        return [jnp.where(first, attend, zero), jnp.where(first, zero, attend)]

    def mixed_rows(norm, spread, p):
        lo, hi = p * two, (p + 1) * two
        return matmul(
            beside([part for hh in range(heads) for part in spread[p, hh]], 0),
            diagonal([norm[lo:hi, lanes(hh)] for hh in range(heads)]),
            0,
            0,
        )

    def backward(b, blk):
        if b + 1 == layers:
            pltpu.make_async_copy(cot.at[blk], cot.at[blk], c_recv.at[blk]).wait()
        else:
            inner = exchanged(layers - 1 + b, blk) * (1.0 / width)
            root = roots[b + 1, blk]
            along = as_column(inner * root * root * root)
            _, gain_row, _ = layer_params(b + 1)
            dy = dnormed[blk].astype(F32) * gain_row
            back = wide(rstd[b + 1, blk]) * dy - xs[b + 1, blk].astype(F32) * wide(along)
        weight, gain_row, scale_row = layer_params(b)
        given = beside([cot[blk, hh] for hh in range(heads)], 1).astype(F32)
        if b + 1 < layers:
            given = (given + back).astype(BF16)
            if b > 0:
                for hh in range(heads):
                    cot[blk, hh] = given[:, lanes(hh)]
            given = given.astype(F32)
            add_tail(1, blk, jnp.sum(given * mixed[b, blk], axis=0, keepdims=True))
        dmix = (given * scale_row).astype(BF16)
        tiles = [(p, hh) for p in range(pairs) for hh in range(heads)]
        datts = []
        for p, hh in tiles:
            lo, mid, hi = p * two, p * two + seq, (p + 1) * two
            datts.append(
                matmul(
                    beside(
                        [normed[b, blk, lo:mid, lanes(hh)], normed[b, blk, mid:hi, lanes(hh)]], 1
                    ),
                    diagonal([dmix[lo:mid, lanes(hh)], dmix[mid:hi, lanes(hh)]]),
                    1,
                    1,
                )
            )
        dscores, attends = {}, {}
        for (p, hh), datt in zip(tiles, datts):
            datt = datt.astype(BF16).astype(F32)
            attend = probs[b, blk, p, hh]
            inner = jnp.sum(datt * attend, axis=0, keepdims=True)
            dscore = (attend * (datt - inner)).astype(BF16)
            attend = attend.astype(BF16)
            zero = jnp.zeros_like(dscore)
            dscores[p, hh] = beside(
                [jnp.where(first, dscore, zero), jnp.where(first, zero, dscore)], 0
            )
            attends[p, hh] = beside(
                [jnp.where(first, attend, zero), jnp.where(first, zero, attend)], 0
            )
        dqueries, dnorms = [], []
        for p in range(pairs):
            lo, hi = p * two, (p + 1) * two
            dquery = matmul(
                beside([dscores[p, hh] for hh in range(heads)], 0),
                diagonal([normed[b, blk, lo:hi, lanes(hh)] for hh in range(heads)]),
                0,
                0,
            )
            dqueries.append(dquery.astype(BF16))
            dnorms.append(
                beside(
                    [
                        matmul(
                            beside([dscores[p, hh], attends[p, hh]], 1),
                            beside(
                                [
                                    queries[b, blk, lo:hi, lanes(hh)],
                                    dmix[lo:hi, lanes(hh)],
                                ],
                                0,
                            ),
                            1,
                            0,
                        )
                        for hh in range(heads)
                    ],
                    1,
                )
            )
        dquery = beside(dqueries, 0)

        if b == 0:
            for hh in range(heads):
                grad = matmul(normed[b, blk, :, lanes(hh)], dquery[:, lanes(hh)], 0, 0)
                if blk > 0:
                    grad = grad + grads[hh]
                grads[hh] = grad
            if blk + 1 == BLOCKS:
                send_grads(b)
        else:
            dqueried[blk] = dquery
        dnorm = beside(dnorms, 0) + matmul(dquery, weight, 1, 1) * inv
        dnorm = dnorm.astype(BF16)
        if b > 0:
            dnormed[blk] = dnorm
            x_in = xs[b, blk].astype(F32)
            exchange(layers - 2 + b, blk, both(dnorm.astype(F32) * gain_row * x_in))
        else:
            add_gain(b, blk, dnorm)
            if blk + 1 == BLOCKS:
                send_tails(b)

    def add_tail(row, blk, part):
        if blk > 0:
            part = part + tails[row : row + 1]
        tails[row : row + 1] = part

    def add_gain(b, blk, dnorm):
        unit = xs[b, blk].astype(F32) * wide(rstd[b, blk])
        add_tail(0, blk, jnp.sum(dnorm.astype(F32) * unit, axis=0, keepdims=True))

    def later_grads(b):
        for hh in range(heads):
            grads[hh] = matmul(
                beside([normed[b, blk, :, lanes(hh)] for blk in range(BLOCKS)], 0),
                beside([dqueried[blk, :, lanes(hh)] for blk in range(BLOCKS)], 0),
                0,
                0,
            )
        send_grads(b)

    def later_tails(b):
        for blk in range(BLOCKS):
            add_gain(b, blk, dnormed[blk])
            if b + 1 < layers:
                continue
            norm = normed[b, blk]
            spread = {
                (p, hh): spread_out(probs[b, blk, p, hh])
                for p in range(pairs)
                for hh in range(heads)
            }
            mix = beside([mixed_rows(norm, spread, p) for p in range(pairs)], 0)
            given = beside([cot[blk, hh] for hh in range(heads)], 1).astype(F32)
            add_tail(1, blk, jnp.sum(given * mix, axis=0, keepdims=True))
        send_tails(b)

    def give_grads(b, source, target, sent, arrived):
        for hh in range(heads):
            for i in range(per_head):
                at = hh * per_head + i
                r = head_of(me_p, me_s, hh) * per_head + i
                mine = (r == me_d) & (me_s == b)

                @pl.when(mine)
                def _():
                    pltpu.make_async_copy(source.at[b, at], target.at[me_z], arrived).start()

                @pl.when(jnp.logical_not(mine))
                def _():
                    remote(source.at[b, at], target.at[me_z], sent, arrived, r, b).start()

    def send_grads(b):
        for hh in range(heads):
            dweight = (grads[hh] * inv).astype(BF16)
            for i in range(per_head):
                tx[b, hh * per_head + i] = dweight[i * rows : (i + 1) * rows]
        give_grads(b, tx, rx, g_send, g_recv)

    def send_tails(b):
        for hh in range(heads):
            gain_part, scale_part = tails[0:1, lanes(hh)], tails[1:2, lanes(hh)]
            gain_hi = gain_part.astype(BF16).astype(F32)
            scale_hi = scale_part.astype(BF16).astype(F32)
            tail = jnp.where(
                tail_row == 0,
                gain_hi,
                jnp.where(
                    tail_row == 1,
                    gain_part - gain_hi,
                    jnp.where(
                        tail_row == 2,
                        scale_hi,
                        jnp.where(tail_row == 3, scale_part - scale_hi, 0.0),
                    ),
                ),
            ).astype(BF16)
            for i in range(per_head):
                tail_tx[b, hh * per_head + i] = tail
        give_grads(b, tail_tx, tail_rx, tg_send, tg_recv)

    pltpu.make_async_copy(tbl, tbl, load_sem).wait()
    chunk = math.gcd(vocab, 128)

    def table_norm(i, carry):
        at = pl.ds(pl.multiple_of(i * chunk, chunk), chunk)
        squares = jnp.zeros((chunk, hd), F32)
        for h in range(width // hd):
            block = tbl[at, h * hd : (h + 1) * hd].astype(F32)
            squares = squares + block * block
        table_rstd[:, at] = lax.rsqrt(as_row(squares) * (1.0 / width) + 1e-05)
        return carry

    lax.fori_loop(0, vocab // chunk, table_norm, 0)

    for load in own_columns:
        load.wait()
    if plane > 1:
        pltpu.make_async_copy(
            toks.at[pl.ds(0, plane - 1)], toks.at[pl.ds(0, plane - 1)], t_recv
        ).wait()
    embed(0)
    pl.when(me_s > 0)(give_all)
    for b in range(layers):
        pltpu.make_async_copy(params.at[b], params.at[b], w_recv.at[b]).wait()
        for blk in range(BLOCKS):
            if b == 0 and blk > 0:
                embed(blk)
            forward(b, blk)
            if b == 0:
                send_cot(BLOCKS - 1, cuts[blk + 1], cuts[blk + 2])
            if b + 1 == layers:
                backward(b, blk)
    for b in reversed(range(layers - 1)):
        later_grads(b + 1)
        later_tails(b + 1)
        for blk in range(BLOCKS):
            backward(b, blk)

    pltpu.make_async_copy(rx, rx, g_recv).wait()
    total_query = jnp.sum(rx[...].astype(F32), axis=0)
    query_squares = jnp.sum(total_query * total_query, axis=0, keepdims=True)
    pltpu.make_async_copy(tail_rx, tail_rx, tg_recv).wait()
    total = jnp.sum(tail_rx[...].astype(F32), axis=0)
    total_gain = total[0:1] + total[1:2]
    total_scale = total[2:3] + total[3:4]
    if per_head > 1:
        at = lax.broadcasted_iota(jnp.int32, (1, hd), 1)
        start = lax.rem(me_d, per_head) * rows
        inside = (at >= start) & (at < start + rows)
        total_gain = jnp.where(inside, total_gain, 0.0)
        total_scale = jnp.where(inside, total_scale, 0.0)
    squares = (
        query_squares
        + total_gain * total_gain
        + total_scale * total_scale
    )
    norms[pl.ds(me, 1)] = squares[None]

    def tell(d, s):
        remote(norms.at[me], norms.at[me], n_send, n_recv, d, s).start()

    peers(n_dp, me_d, tell)

    if members > 1:
        for phase in range(2 * layers - 2):
            whole = parts.at[phase, :, pl.ds(0, members - 1)]
            pltpu.make_async_copy(whole, whole, x_send).wait()
    if plane > 1:
        sent = toks.at[pl.ds(0, plane - 1)]
        pltpu.make_async_copy(sent, sent, t_send).wait()
        sent = cot.at[:, :, pl.ds(0, (plane - 1) * some)]
        pltpu.make_async_copy(sent, sent, c_send).wait()

    def sent_weight(k, carry):
        pltpu.make_async_copy(packed, packed, w_send).wait()
        return carry

    lax.fori_loop(0, jnp.where(keep, planes - 1, planes), sent_weight, 0)

    def sent_grad(k, carry):
        pltpu.make_async_copy(rx.at[0], rx.at[0], g_send).wait()
        pltpu.make_async_copy(tail_rx.at[0], tail_rx.at[0], tg_send).wait()
        return carry

    pieces = layers * heads * per_head
    lax.fori_loop(0, jnp.where(keep, pieces - 1, pieces), sent_grad, 0)

    others = norms.at[pl.ds(0, n_dev - 1)]
    pltpu.make_async_copy(others, others, n_recv).wait()
    overall = jnp.sum(jnp.sum(norms[...], axis=0), axis=1, keepdims=True)
    limit = float(layers * width * (hd + 2))
    factor = jnp.minimum(1.0, math.sqrt(limit) / jnp.sqrt(overall))
    out[0:rows] = total_query * factor
    out[rows : rows + 8] = jnp.where(
        lax.broadcasted_iota(jnp.int32, (8, hd), 0) == 0, total_gain * factor, total_scale * factor
    )
    pltpu.make_async_copy(others, others, n_send).wait()


def split_kernel(found, query_grad, gain_grad, scale_grad):
    rows = query_grad.shape[0]
    query_grad[...] = found[0:rows]
    gain_grad[...] = found[rows : rows + 1]
    scale_grad[...] = found[rows + 1 : rows + 2]


def on_device(path_table, tokens, assign, out_grad, query_weights, gain, scale):
    n_dp = lax.axis_size("dp")
    n_sec = lax.axis_size("section")
    vocab, width = path_table.shape
    slots, seq = tokens.shape[1:]
    rows, hd = query_weights.shape[1:]
    count = slots * seq
    layers = n_sec
    plane, planes, heads = layout(n_dp, n_sec, width, hd)
    per_head = hd // rows
    pieces = heads * per_head
    n_dev = n_dp * n_sec
    held = heads * hd
    block_rows = plane * count // BLOCKS
    pairs = block_rows // (2 * seq)
    phases = max(1, 2 * layers - 2)
    first = lax.rem(lax.axis_index("dp") * rows, hd)
    if rows < hd:
        gain = lax.dynamic_update_slice(jnp.zeros((1, hd), BF16), gain, (0, first))
        scale = lax.dynamic_update_slice(jnp.zeros((1, hd), BF16), scale, (0, first))
    vmem = pl.BlockSpec(memory_space=pltpu.VMEM)
    hbm = pl.BlockSpec(memory_space=pl.ANY)
    stream = pltpu.VMEM((layers, BLOCKS, block_rows, held), BF16)
    found = pl.pallas_call(
        functools.partial(step_kernel, n_dp, n_sec),
        out_shape=pltpu.VMEM((rows + 8, hd), F32),
        in_specs=[hbm] * 7,
        out_specs=vmem,
        scratch_shapes=[
            pltpu.VMEM((slots, seq), jnp.int32),
            pltpu.SMEM((slots,), jnp.int32),
            pltpu.VMEM((1, hd), BF16),
            pltpu.VMEM((1, hd), BF16),
            pltpu.VMEM((rows + TAIL, hd), BF16),
            pltpu.VMEM((layers, pieces, rows + TAIL, hd), BF16),
            pltpu.VMEM((plane, 1, count), F32),
            pltpu.VMEM((vocab, width), BF16),
            pltpu.VMEM((vocab, held), BF16),
            pltpu.VMEM((block_rows, vocab), BF16),
            pltpu.VMEM((1, vocab), F32),
            pltpu.VMEM((BLOCKS, heads, block_rows, hd), BF16),
            stream,
            stream,
            stream,
            pltpu.VMEM((layers, BLOCKS, block_rows, held), F32),
            pltpu.VMEM((layers, BLOCKS, pairs, heads, seq, 2 * seq), F32),
            pltpu.VMEM((BLOCKS, block_rows, held), BF16),
            pltpu.VMEM((BLOCKS, block_rows, held), BF16),
            pltpu.VMEM((layers, BLOCKS, block_rows, hd), F32),
            pltpu.VMEM((layers, BLOCKS, 1, block_rows), F32),
            pltpu.VMEM((phases, BLOCKS, plane * n_sec, 1, block_rows), F32),
            pltpu.VMEM((heads, hd, hd), F32),
            pltpu.VMEM((8, held), F32),
            pltpu.VMEM((layers, pieces, rows, hd), BF16),
            pltpu.VMEM((planes, rows, hd), BF16),
            pltpu.VMEM((layers, pieces, TAIL, hd), BF16),
            pltpu.VMEM((planes, TAIL, hd), BF16),
            pltpu.VMEM((n_dev, 1, hd), F32),
            pltpu.SemaphoreType.DMA((5,)),
            pltpu.SemaphoreType.DMA,
            pltpu.SemaphoreType.DMA((heads,)),
            pltpu.SemaphoreType.DMA,
            pltpu.SemaphoreType.DMA,
            pltpu.SemaphoreType.DMA,
            pltpu.SemaphoreType.DMA((layers,)),
            pltpu.SemaphoreType.DMA,
            pltpu.SemaphoreType.DMA((BLOCKS,)),
            pltpu.SemaphoreType.DMA,
            pltpu.SemaphoreType.DMA((phases, BLOCKS)),
            pltpu.SemaphoreType.DMA,
            pltpu.SemaphoreType.DMA,
            pltpu.SemaphoreType.DMA,
            pltpu.SemaphoreType.DMA,
            pltpu.SemaphoreType.DMA,
            pltpu.SemaphoreType.DMA,
        ],
        compiler_params=pltpu.CompilerParams(
            collective_id=0, has_side_effects=True, vmem_limit_bytes=56 * 1024 * 1024
        ),
    )(
        path_table,
        tokens[0],
        assign[0],
        out_grad.reshape(count, width),
        query_weights[0],
        gain,
        scale,
    )
    query_grad, gain_grad, scale_grad = pl.pallas_call(
        split_kernel,
        out_shape=(
            jax.ShapeDtypeStruct((rows, hd), F32),
            jax.ShapeDtypeStruct((1, hd), F32),
            jax.ShapeDtypeStruct((1, hd), F32),
        ),
        in_specs=[vmem],
        out_specs=(vmem, vmem, vmem),
        compiler_params=pltpu.CompilerParams(vmem_limit_bytes=1024 * 1024),
    )(found)
    if rows < hd:
        gain_grad = lax.dynamic_slice(gain_grad, (0, first), (1, rows))
        scale_grad = lax.dynamic_slice(scale_grad, (0, first), (1, rows))
    return query_grad[None], gain_grad, scale_grad


def solution(mesh):
    in_specs = (
        P(),
        P("dp", None, None),
        P("dp", None),
        P("dp", None, None, None, None),
        P("section", "dp", None),
        P("section", "dp"),
        P("section", "dp"),
    )
    out_specs = (P("section", "dp", None), P("section", "dp"), P("section", "dp"))
    return jax.shard_map(
        on_device, mesh=mesh, in_specs=in_specs, out_specs=out_specs, check_vma=False
    )
```

```python
import functools
import math

import jax
import jax.numpy as jnp
from jax import lax
from jax.experimental import pallas as pl
from jax.experimental.pallas import tpu as pltpu
from jax.sharding import PartitionSpec as P

MESH = pl.DeviceIdType.MESH
F32 = jnp.float32
BF16 = jnp.bfloat16
TAIL = 16
PLANE = 4
BLOCKS = 2
SHARES = (2, 4, 6)
UNROLL = 32


def matmul(lhs, rhs, lhs_dim, rhs_dim):
    return lax.dot_general(
        lhs, rhs, (((lhs_dim,), (rhs_dim,)), ((), ())), preferred_element_type=F32
    )


def beside(parts, axis):
    return parts[0] if len(parts) == 1 else jnp.concatenate(parts, axis=axis)


def diagonal(parts):
    zero = jnp.zeros_like(parts[0])
    return beside(
        [
            beside([part if i == k else zero for k in range(len(parts))], 1)
            for i, part in enumerate(parts)
        ],
        0,
    )


def layout(n_dp, n_sec, width, hd):
    plane = math.gcd(n_dp, min(PLANE, width // hd // n_sec))
    return plane, n_dp // plane, width // hd // n_sec // plane


def step_kernel(
    n_dp,
    n_sec,
    table,
    tokens,
    assign,
    out_grad,
    weights,
    gain,
    scale,
    out,
    tokens_in,
    assign_in,
    gain_in,
    scale_in,
    packed,
    params,
    toks,
    tbl,
    emb,
    picked,
    table_rstd,
    cot,
    xs,
    normed,
    queries,
    mixed,
    probs,
    dnormed,
    dqueried,
    rstd,
    roots,
    parts,
    grads,
    tails,
    tx,
    rx,
    tail_tx,
    tail_rx,
    norms,
    in_sem,
    load_sem,
    emb_sem,
    t_send,
    t_recv,
    w_send,
    w_recv,
    c_send,
    c_recv,
    x_send,
    x_recv,
    g_send,
    g_recv,
    tg_send,
    tg_recv,
    n_send,
    n_recv,
):
    slots, seq = tokens.shape
    vocab, width = table.shape
    rows, hd = weights.shape
    plane, planes, heads = layout(n_dp, n_sec, width, hd)
    layers = n_sec
    per_head = hd // rows
    n_dev = n_dp * n_sec
    members = plane * n_sec
    held = heads * hd
    some = slots // BLOCKS * seq
    block_rows = plane * some
    two = 2 * seq
    pairs = block_rows // two
    inv = 1.0 / math.sqrt(hd)
    me_d = lax.axis_index("dp")
    me_s = lax.axis_index("section")
    me = me_d * n_sec + me_s
    me_z = lax.div(me_d, plane)
    me_p = lax.rem(me_d, plane)
    member = me_p * n_sec + me_s

    def repeat(first, last, body):
        if last - first <= UNROLL:
            for k in range(first, last):
                body(k)
        else:

            def step(k, carry):
                body(k)
                return carry

            lax.fori_loop(first, last, step, 0)

    def after(at, k, size):
        moved = at + k
        return jnp.where(moved >= size, moved - size, moved)

    def peers(size, at, body):
        if size * n_sec <= UNROLL:
            for kd in [*range(size // 2, size), *reversed(range(size // 2))]:
                d = after(at, kd, size) if kd else at
                for ks in range(n_sec):
                    if kd or ks:
                        body(d, after(me_s, ks, n_sec) if ks else me_s)
        else:

            def step(k, carry):
                t = lax.rem(at * n_sec + me_s + k, size * n_sec)
                body(lax.div(t, n_sec), lax.rem(t, n_sec))
                return carry

            lax.fori_loop(1, size * n_sec, step, 0)

    def head_of(p, c, hh):
        return (c * heads + hh) * plane + p

    def columns(h):
        return pl.ds(pl.multiple_of(h * hd, hd), hd)

    def lanes(hh):
        return slice(hh * hd, (hh + 1) * hd)

    def remote(src, dst, ssem, rsem, d, s):
        return pltpu.make_async_remote_copy(
            src_ref=src,
            dst_ref=dst,
            send_sem=ssem,
            recv_sem=rsem,
            device_id=(d, s),
            device_id_type=MESH,
        )

    barrier = pltpu.get_barrier_semaphore()

    def greet(d, s):
        pl.semaphore_signal(barrier, inc=1, device_id=(d, s), device_id_type=MESH)

    peers(n_dp, me_d, greet)
    pltpu.make_async_copy(table, tbl, load_sem).start()
    loads = [
        pltpu.make_async_copy(tokens, tokens_in, in_sem.at[0]),
        pltpu.make_async_copy(assign, assign_in, in_sem.at[1]),
        pltpu.make_async_copy(weights, packed.at[pl.ds(0, rows)], in_sem.at[2]),
        pltpu.make_async_copy(gain, gain_in, in_sem.at[3]),
        pltpu.make_async_copy(scale, scale_in, in_sem.at[4]),
    ]
    for load in loads:
        load.start()
    own_columns = [
        pltpu.make_async_copy(
            table.at[:, columns(head_of(me_p, me_s, hh))], emb.at[:, lanes(hh)], emb_sem.at[hh]
        )
        for hh in range(heads)
    ]
    for load in own_columns:
        load.start()

    def cot_at(blk, p, hh, start, size):
        return cot.at[blk, hh, pl.ds(p * some + start, size)]

    def cot_from(blk, h, start, size):
        return out_grad.at[pl.ds(blk * some + start, size), columns(h)]

    for blk in range(BLOCKS):
        for hh in range(heads):
            pltpu.make_async_copy(
                cot_from(blk, head_of(me_p, me_s, hh), 0, some),
                cot_at(blk, me_p, hh, 0, some),
                c_recv.at[blk],
            ).start()

    for load in loads:
        load.wait()
    tail_row = lax.broadcasted_iota(jnp.int32, (TAIL, hd), 0)
    packed[rows : rows + TAIL, :] = jnp.where(
        tail_row == 0,
        gain_in[...].astype(F32),
        jnp.where(tail_row == 1, scale_in[...].astype(F32), 0.0),
    ).astype(BF16)
    toks[me_p] = beside(
        [tokens_in[pl.ds(assign_in[j], 1), :].astype(F32) for j in range(slots)], 1
    )

    pl.semaphore_wait(barrier, n_dev - 1)

    my_head = lax.div(me_d * rows, hd)
    to_p = lax.rem(my_head, plane)
    to_i = lax.div(my_head, plane)
    to_s = lax.div(to_i, heads)
    place = lax.rem(to_i, heads) * per_head + lax.rem(me_d, per_head)
    keep = (to_p == me_p) & (to_s == me_s)

    def give(k):
        z = lax.rem(me_z + k, planes)
        remote(
            packed, params.at[me_s, place], w_send, w_recv.at[me_s], z * plane + to_p, to_s
        ).start()

    def give_all():
        repeat(1, planes, give)

        @pl.when(keep)
        def _():
            pltpu.make_async_copy(packed, params.at[me_s, place], w_recv.at[me_s]).start()

        @pl.when(jnp.logical_not(keep))
        def _():
            remote(
                packed,
                params.at[me_s, place],
                w_send,
                w_recv.at[me_s],
                me_z * plane + to_p,
                to_s,
            ).start()

    for k in range(1, plane):
        p = lax.rem(me_p + k, plane)
        remote(toks.at[me_p], toks.at[me_p], t_send, t_recv, me_z * plane + p, me_s).start()

    pl.when(me_s == 0)(give_all)

    cuts = [sum(SHARES[:k]) * (some // 16) // sum(SHARES) * 16 for k in range(len(SHARES))]
    cuts.append(some)

    def send_cot(blk, begin, end):
        if begin == end:
            return
        for k in range(1, plane):
            p = lax.rem(me_p + k, plane)
            for hh in range(heads):
                remote(
                    cot_from(blk, head_of(p, me_s, hh), begin, end - begin),
                    cot_at(blk, me_p, hh, begin, end - begin),
                    c_send,
                    c_recv.at[blk],
                    me_z * plane + p,
                    me_s,
                ).start()

    for blk in range(BLOCKS - 1):
        send_cot(blk, 0, some)
    send_cot(BLOCKS - 1, cuts[0], cuts[1])

    ones_row = jnp.ones((TAIL, 2 * hd), BF16)
    ones_column = jnp.ones((TAIL, hd), BF16)

    def as_row(terms):
        high = terms.astype(BF16)
        low = (terms - high.astype(F32)).astype(BF16)
        return matmul(ones_row, beside([high, low], 1), 1, 1)[0:1]

    def as_column(row):
        at = lax.broadcasted_iota(jnp.int32, (TAIL, row.shape[1]), 0)
        high = row.astype(BF16).astype(F32)
        mid = (row - high).astype(BF16).astype(F32)
        low = row - high - mid
        stack = jnp.where(at == 0, high, jnp.where(at == 1, mid, jnp.where(at == 2, low, 0.0)))
        return matmul(stack.astype(BF16), ones_column, 0, 0)

    def exchange(phase, blk, terms):
        parts[phase, blk, member] = as_row(terms)

        def share(p, s):
            remote(
                parts.at[phase, blk, member],
                parts.at[phase, blk, member],
                x_send,
                x_recv.at[phase, blk],
                me_z * plane + p,
                s,
            ).start()

        peers(plane, me_p, share)

    def exchanged(phase, blk):
        if members > 1:
            whole = parts.at[phase, blk, pl.ds(0, members - 1)]
            pltpu.make_async_copy(whole, whole, x_recv.at[phase, blk]).wait()
        return jnp.sum(parts[phase, blk], axis=0)

    def layer_param(b, hh):
        at = hh * per_head
        tail = params[b, at, rows:, :].astype(F32)
        weight = params[b, at, :rows, :]
        if per_head > 1:
            for i in range(1, per_head):
                tail = tail + params[b, at + i, rows:, :].astype(F32)
            weight = jnp.concatenate(
                [params[b, at + i, :rows, :] for i in range(per_head)], axis=0
            )
        return weight, tail[0:1], tail[1:2]

    def layer_params(b):
        found = [layer_param(b, hh) for hh in range(heads)]
        return (
            diagonal([one[0] for one in found]),
            beside([one[1] for one in found], 1),
            beside([one[2] for one in found], 1),
        )

    at_row = lax.broadcasted_iota(jnp.int32, (seq, two), 0)
    at_col = lax.broadcasted_iota(jnp.int32, (seq, two), 1)
    first = at_col < seq
    allowed = at_row <= jnp.where(first, at_col, at_col - seq)
    vocab_lane = lax.broadcasted_iota(jnp.int32, (some, hd), 1).astype(F32)

    def wide(column):
        return beside([column] * heads, 1)

    def both(sides):
        return sides[:, :hd] if heads == 1 else sum(sides[:, lanes(hh)] for hh in range(heads))

    def embed(blk):
        for p in range(plane):
            col = as_column(toks[p, :, blk * some : (blk + 1) * some])
            at = slice(p * some, (p + 1) * some)
            root = jnp.zeros((some, hd), F32)
            for v in range(vocab // hd):
                hit = vocab_lane + float(v * hd) == col
                picked[at, lanes(v)] = jnp.where(hit, 1.0, 0.0).astype(BF16)
                root = root + jnp.where(hit, table_rstd[:, lanes(v)], 0.0)
            rstd[0, blk, at] = jnp.broadcast_to(jnp.sum(root, axis=1, keepdims=True), (some, hd))
        xs[0, blk] = matmul(picked[...], emb[...], 1, 0).astype(BF16)

    def forward(b, blk):
        if b > 0:
            root = lax.rsqrt(exchanged(b - 1, blk) * (1.0 / width) + 1e-05)
            roots[b, blk] = root
            rstd[b, blk] = as_column(root)
        weight, gain_row, scale_row = layer_params(b)
        norm = (xs[b, blk].astype(F32) * wide(rstd[b, blk]) * gain_row).astype(BF16)
        normed[b, blk] = norm
        query = (matmul(norm, weight, 1, 0) * inv).astype(BF16)
        queries[b, blk] = query
        tiles = [(p, hh) for p in range(pairs) for hh in range(heads)]
        scores = []
        for p, hh in tiles:
            lo, mid, hi = p * two, p * two + seq, (p + 1) * two
            scores.append(
                matmul(
                    beside([norm[lo:mid, lanes(hh)], norm[mid:hi, lanes(hh)]], 1),
                    diagonal([query[lo:mid, lanes(hh)], query[mid:hi, lanes(hh)]]),
                    1,
                    1,
                )
            )
        spread = {}
        for (p, hh), score in zip(tiles, scores):
            score = jnp.where(allowed, score, -1e30)
            raised = jnp.exp(score - jnp.max(score, axis=0, keepdims=True))
            attend = raised * (1.0 / jnp.sum(raised, axis=0, keepdims=True))
            probs[b, blk, p, hh] = attend
            if b + 1 < layers:
                spread[p, hh] = spread_out(attend)
        if b + 1 == layers:
            return
        terms = []
        for p in range(pairs):
            lo, hi = p * two, (p + 1) * two
            mix = mixed_rows(norm, spread, p)
            mixed[b, blk, lo:hi] = mix
            out_rows = (xs[b, blk, lo:hi].astype(F32) + scale_row * mix).astype(BF16)
            xs[b + 1, blk, lo:hi] = out_rows
            out_rows = out_rows.astype(F32)
            terms.append(both(out_rows * out_rows))
        exchange(b, blk, beside(terms, 0))

    def spread_out(attend):
        attend = attend.astype(BF16)
        zero = jnp.zeros_like(attend)
        return [jnp.where(first, attend, zero), jnp.where(first, zero, attend)]

    def mixed_rows(norm, spread, p):
        lo, hi = p * two, (p + 1) * two
        return matmul(
            beside([part for hh in range(heads) for part in spread[p, hh]], 0),
            diagonal([norm[lo:hi, lanes(hh)] for hh in range(heads)]),
            0,
            0,
        )

    def backward(b, blk):
        if b + 1 == layers:
            pltpu.make_async_copy(cot.at[blk], cot.at[blk], c_recv.at[blk]).wait()
        else:
            inner = exchanged(layers - 1 + b, blk) * (1.0 / width)
            root = roots[b + 1, blk]
            along = as_column(inner * root * root * root)
            _, gain_row, _ = layer_params(b + 1)
            dy = dnormed[blk].astype(F32) * gain_row
            back = wide(rstd[b + 1, blk]) * dy - xs[b + 1, blk].astype(F32) * wide(along)
        weight, gain_row, scale_row = layer_params(b)
        given = beside([cot[blk, hh] for hh in range(heads)], 1).astype(F32)
        if b + 1 < layers:
            given = (given + back).astype(BF16)
            if b > 0:
                for hh in range(heads):
                    cot[blk, hh] = given[:, lanes(hh)]
            given = given.astype(F32)
            add_tail(1, blk, jnp.sum(given * mixed[b, blk], axis=0, keepdims=True))
        dmix = (given * scale_row).astype(BF16)
        tiles = [(p, hh) for p in range(pairs) for hh in range(heads)]
        datts = []
        for p, hh in tiles:
            lo, mid, hi = p * two, p * two + seq, (p + 1) * two
            datts.append(
                matmul(
                    beside(
                        [normed[b, blk, lo:mid, lanes(hh)], normed[b, blk, mid:hi, lanes(hh)]], 1
                    ),
                    diagonal([dmix[lo:mid, lanes(hh)], dmix[mid:hi, lanes(hh)]]),
                    1,
                    1,
                )
            )
        dscores, attends = {}, {}
        for (p, hh), datt in zip(tiles, datts):
            datt = datt.astype(BF16).astype(F32)
            attend = probs[b, blk, p, hh]
            inner = jnp.sum(datt * attend, axis=0, keepdims=True)
            dscore = (attend * (datt - inner)).astype(BF16)
            attend = attend.astype(BF16)
            zero = jnp.zeros_like(dscore)
            dscores[p, hh] = beside(
                [jnp.where(first, dscore, zero), jnp.where(first, zero, dscore)], 0
            )
            attends[p, hh] = beside(
                [jnp.where(first, attend, zero), jnp.where(first, zero, attend)], 0
            )
        dqueries, dnorms = [], []
        for p in range(pairs):
            lo, hi = p * two, (p + 1) * two
            dquery = matmul(
                beside([dscores[p, hh] for hh in range(heads)], 0),
                diagonal([normed[b, blk, lo:hi, lanes(hh)] for hh in range(heads)]),
                0,
                0,
            )
            dqueries.append(dquery.astype(BF16))
            dnorms.append(
                beside(
                    [
                        matmul(
                            beside([dscores[p, hh], attends[p, hh]], 1),
                            beside(
                                [
                                    queries[b, blk, lo:hi, lanes(hh)],
                                    dmix[lo:hi, lanes(hh)],
                                ],
                                0,
                            ),
                            1,
                            0,
                        )
                        for hh in range(heads)
                    ],
                    1,
                )
            )
        dquery = beside(dqueries, 0)

        if b == 0:
            for hh in range(heads):
                grad = matmul(normed[b, blk, :, lanes(hh)], dquery[:, lanes(hh)], 0, 0)
                if blk > 0:
                    grad = grad + grads[hh]
                grads[hh] = grad
            if blk + 1 == BLOCKS:
                send_grads(b)
        else:
            dqueried[blk] = dquery
        dnorm = beside(dnorms, 0) + matmul(dquery, weight, 1, 1) * inv
        dnorm = dnorm.astype(BF16)
        if b > 0:
            dnormed[blk] = dnorm
            x_in = xs[b, blk].astype(F32)
            exchange(layers - 2 + b, blk, both(dnorm.astype(F32) * gain_row * x_in))
        else:
            add_gain(b, blk, dnorm)
            if blk + 1 == BLOCKS:
                send_tails(b)

    def add_tail(row, blk, part):
        if blk > 0:
            part = part + tails[row : row + 1]
        tails[row : row + 1] = part

    def add_gain(b, blk, dnorm):
        unit = xs[b, blk].astype(F32) * wide(rstd[b, blk])
        add_tail(0, blk, jnp.sum(dnorm.astype(F32) * unit, axis=0, keepdims=True))

    def later_grads(b):
        for hh in range(heads):
            grads[hh] = matmul(
                beside([normed[b, blk, :, lanes(hh)] for blk in range(BLOCKS)], 0),
                beside([dqueried[blk, :, lanes(hh)] for blk in range(BLOCKS)], 0),
                0,
                0,
            )
        send_grads(b)

    def later_tails(b):
        for blk in range(BLOCKS):
            add_gain(b, blk, dnormed[blk])
            if b + 1 < layers:
                continue
            norm = normed[b, blk]
            spread = {
                (p, hh): spread_out(probs[b, blk, p, hh])
                for p in range(pairs)
                for hh in range(heads)
            }
            mix = beside([mixed_rows(norm, spread, p) for p in range(pairs)], 0)
            given = beside([cot[blk, hh] for hh in range(heads)], 1).astype(F32)
            add_tail(1, blk, jnp.sum(given * mix, axis=0, keepdims=True))
        send_tails(b)

    def give_grads(b, source, target, sent, arrived):
        for hh in range(heads):
            for i in range(per_head):
                at = hh * per_head + i
                r = head_of(me_p, me_s, hh) * per_head + i
                mine = (r == me_d) & (me_s == b)

                @pl.when(mine)
                def _():
                    pltpu.make_async_copy(source.at[b, at], target.at[me_z], arrived).start()

                @pl.when(jnp.logical_not(mine))
                def _():
                    remote(source.at[b, at], target.at[me_z], sent, arrived, r, b).start()

    def send_grads(b):
        for hh in range(heads):
            dweight = (grads[hh] * inv).astype(BF16)
            for i in range(per_head):
                tx[b, hh * per_head + i] = dweight[i * rows : (i + 1) * rows]
        give_grads(b, tx, rx, g_send, g_recv)

    def send_tails(b):
        for hh in range(heads):
            gain_part, scale_part = tails[0:1, lanes(hh)], tails[1:2, lanes(hh)]
            gain_hi = gain_part.astype(BF16).astype(F32)
            scale_hi = scale_part.astype(BF16).astype(F32)
            tail = jnp.where(
                tail_row == 0,
                gain_hi,
                jnp.where(
                    tail_row == 1,
                    gain_part - gain_hi,
                    jnp.where(
                        tail_row == 2,
                        scale_hi,
                        jnp.where(tail_row == 3, scale_part - scale_hi, 0.0),
                    ),
                ),
            ).astype(BF16)
            for i in range(per_head):
                tail_tx[b, hh * per_head + i] = tail
        give_grads(b, tail_tx, tail_rx, tg_send, tg_recv)

    pltpu.make_async_copy(tbl, tbl, load_sem).wait()
    chunk = math.gcd(vocab, 128)

    def table_norm(i, carry):
        at = pl.ds(pl.multiple_of(i * chunk, chunk), chunk)
        squares = jnp.zeros((chunk, hd), F32)
        for h in range(width // hd):
            block = tbl[at, h * hd : (h + 1) * hd].astype(F32)
            squares = squares + block * block
        table_rstd[:, at] = lax.rsqrt(as_row(squares) * (1.0 / width) + 1e-05)
        return carry

    lax.fori_loop(0, vocab // chunk, table_norm, 0)

    for load in own_columns:
        load.wait()
    if plane > 1:
        pltpu.make_async_copy(
            toks.at[pl.ds(0, plane - 1)], toks.at[pl.ds(0, plane - 1)], t_recv
        ).wait()
    embed(0)
    pl.when(me_s > 0)(give_all)
    for b in range(layers):
        pltpu.make_async_copy(params.at[b], params.at[b], w_recv.at[b]).wait()
        for blk in range(BLOCKS):
            if b == 0 and blk > 0:
                embed(blk)
            forward(b, blk)
            if b == 0:
                send_cot(BLOCKS - 1, cuts[blk + 1], cuts[blk + 2])
            if b + 1 == layers:
                backward(b, blk)
    for b in reversed(range(layers - 1)):
        later_grads(b + 1)
        later_tails(b + 1)
        for blk in range(BLOCKS):
            backward(b, blk)

    pltpu.make_async_copy(rx, rx, g_recv).wait()
    total_query = jnp.sum(rx[...].astype(F32), axis=0)
    query_squares = jnp.sum(total_query * total_query, axis=0, keepdims=True)
    pltpu.make_async_copy(tail_rx, tail_rx, tg_recv).wait()
    total = jnp.sum(tail_rx[...].astype(F32), axis=0)
    total_gain = total[0:1] + total[1:2]
    total_scale = total[2:3] + total[3:4]
    if per_head > 1:
        at = lax.broadcasted_iota(jnp.int32, (1, hd), 1)
        start = lax.rem(me_d, per_head) * rows
        inside = (at >= start) & (at < start + rows)
        total_gain = jnp.where(inside, total_gain, 0.0)
        total_scale = jnp.where(inside, total_scale, 0.0)
    squares = (
        query_squares
        + total_gain * total_gain
        + total_scale * total_scale
    )
    norms[pl.ds(me, 1)] = squares[None]

    def tell(d, s):
        remote(norms.at[me], norms.at[me], n_send, n_recv, d, s).start()

    peers(n_dp, me_d, tell)

    if members > 1:
        for phase in range(2 * layers - 2):
            whole = parts.at[phase, :, pl.ds(0, members - 1)]
            pltpu.make_async_copy(whole, whole, x_send).wait()
    if plane > 1:
        sent = toks.at[pl.ds(0, plane - 1)]
        pltpu.make_async_copy(sent, sent, t_send).wait()
        sent = cot.at[:, :, pl.ds(0, (plane - 1) * some)]
        pltpu.make_async_copy(sent, sent, c_send).wait()

    def sent_weight(k, carry):
        pltpu.make_async_copy(packed, packed, w_send).wait()
        return carry

    lax.fori_loop(0, jnp.where(keep, planes - 1, planes), sent_weight, 0)

    def sent_grad(k, carry):
        pltpu.make_async_copy(rx.at[0], rx.at[0], g_send).wait()
        pltpu.make_async_copy(tail_rx.at[0], tail_rx.at[0], tg_send).wait()
        return carry

    pieces = layers * heads * per_head
    lax.fori_loop(0, jnp.where(keep, pieces - 1, pieces), sent_grad, 0)

    others = norms.at[pl.ds(0, n_dev - 1)]
    pltpu.make_async_copy(others, others, n_recv).wait()
    overall = jnp.sum(jnp.sum(norms[...], axis=0), axis=1, keepdims=True)
    limit = float(layers * width * (hd + 2))
    factor = jnp.minimum(1.0, math.sqrt(limit) / jnp.sqrt(overall))
    out[0:rows] = total_query * factor
    out[rows : rows + 8] = jnp.where(
        lax.broadcasted_iota(jnp.int32, (8, hd), 0) == 0, total_gain * factor, total_scale * factor
    )
    pltpu.make_async_copy(others, others, n_send).wait()


def split_kernel(found, query_grad, gain_grad, scale_grad):
    rows = query_grad.shape[0]
    query_grad[...] = found[0:rows]
    gain_grad[...] = found[rows : rows + 1]
    scale_grad[...] = found[rows + 1 : rows + 2]


def on_device(path_table, tokens, assign, out_grad, query_weights, gain, scale):
    n_dp = lax.axis_size("dp")
    n_sec = lax.axis_size("section")
    vocab, width = path_table.shape
    slots, seq = tokens.shape[1:]
    rows, hd = query_weights.shape[1:]
    count = slots * seq
    layers = n_sec
    plane, planes, heads = layout(n_dp, n_sec, width, hd)
    per_head = hd // rows
    pieces = heads * per_head
    n_dev = n_dp * n_sec
    held = heads * hd
    block_rows = plane * count // BLOCKS
    pairs = block_rows // (2 * seq)
    phases = max(1, 2 * layers - 2)
    first = lax.rem(lax.axis_index("dp") * rows, hd)
    if rows < hd:
        gain = lax.dynamic_update_slice(jnp.zeros((1, hd), BF16), gain, (0, first))
        scale = lax.dynamic_update_slice(jnp.zeros((1, hd), BF16), scale, (0, first))
    vmem = pl.BlockSpec(memory_space=pltpu.VMEM)
    hbm = pl.BlockSpec(memory_space=pl.ANY)
    stream = pltpu.VMEM((layers, BLOCKS, block_rows, held), BF16)
    found = pl.pallas_call(
        functools.partial(step_kernel, n_dp, n_sec),
        out_shape=pltpu.VMEM((rows + 8, hd), F32),
        in_specs=[hbm] * 7,
        out_specs=vmem,
        scratch_shapes=[
            pltpu.VMEM((slots, seq), jnp.int32),
            pltpu.SMEM((slots,), jnp.int32),
            pltpu.VMEM((1, hd), BF16),
            pltpu.VMEM((1, hd), BF16),
            pltpu.VMEM((rows + TAIL, hd), BF16),
            pltpu.VMEM((layers, pieces, rows + TAIL, hd), BF16),
            pltpu.VMEM((plane, 1, count), F32),
            pltpu.VMEM((vocab, width), BF16),
            pltpu.VMEM((vocab, held), BF16),
            pltpu.VMEM((block_rows, vocab), BF16),
            pltpu.VMEM((1, vocab), F32),
            pltpu.VMEM((BLOCKS, heads, block_rows, hd), BF16),
            stream,
            stream,
            stream,
            pltpu.VMEM((layers, BLOCKS, block_rows, held), F32),
            pltpu.VMEM((layers, BLOCKS, pairs, heads, seq, 2 * seq), F32),
            pltpu.VMEM((BLOCKS, block_rows, held), BF16),
            pltpu.VMEM((BLOCKS, block_rows, held), BF16),
            pltpu.VMEM((layers, BLOCKS, block_rows, hd), F32),
            pltpu.VMEM((layers, BLOCKS, 1, block_rows), F32),
            pltpu.VMEM((phases, BLOCKS, plane * n_sec, 1, block_rows), F32),
            pltpu.VMEM((heads, hd, hd), F32),
            pltpu.VMEM((8, held), F32),
            pltpu.VMEM((layers, pieces, rows, hd), BF16),
            pltpu.VMEM((planes, rows, hd), BF16),
            pltpu.VMEM((layers, pieces, TAIL, hd), BF16),
            pltpu.VMEM((planes, TAIL, hd), BF16),
            pltpu.VMEM((n_dev, 1, hd), F32),
            pltpu.SemaphoreType.DMA((5,)),
            pltpu.SemaphoreType.DMA,
            pltpu.SemaphoreType.DMA((heads,)),
            pltpu.SemaphoreType.DMA,
            pltpu.SemaphoreType.DMA,
            pltpu.SemaphoreType.DMA,
            pltpu.SemaphoreType.DMA((layers,)),
            pltpu.SemaphoreType.DMA,
            pltpu.SemaphoreType.DMA((BLOCKS,)),
            pltpu.SemaphoreType.DMA,
            pltpu.SemaphoreType.DMA((phases, BLOCKS)),
            pltpu.SemaphoreType.DMA,
            pltpu.SemaphoreType.DMA,
            pltpu.SemaphoreType.DMA,
            pltpu.SemaphoreType.DMA,
            pltpu.SemaphoreType.DMA,
            pltpu.SemaphoreType.DMA,
        ],
        compiler_params=pltpu.CompilerParams(
            collective_id=0, has_side_effects=True, vmem_limit_bytes=56 * 1024 * 1024
        ),
    )(
        path_table,
        tokens[0],
        assign[0],
        out_grad.reshape(count, width),
        query_weights[0],
        gain,
        scale,
    )
    query_grad, gain_grad, scale_grad = pl.pallas_call(
        split_kernel,
        out_shape=(
            jax.ShapeDtypeStruct((rows, hd), F32),
            jax.ShapeDtypeStruct((1, hd), F32),
            jax.ShapeDtypeStruct((1, hd), F32),
        ),
        in_specs=[vmem],
        out_specs=(vmem, vmem, vmem),
        compiler_params=pltpu.CompilerParams(vmem_limit_bytes=1024 * 1024),
    )(found)
    if rows < hd:
        gain_grad = lax.dynamic_slice(gain_grad, (0, first), (1, rows))
        scale_grad = lax.dynamic_slice(scale_grad, (0, first), (1, rows))
    return query_grad[None], gain_grad, scale_grad


def solution(mesh):
    in_specs = (
        P(),
        P("dp", None, None),
        P("dp", None),
        P("dp", None, None, None, None),
        P("section", "dp", None),
        P("section", "dp"),
        P("section", "dp"),
    )
    out_specs = (P("section", "dp", None), P("section", "dp"), P("section", "dp"))
    return jax.shard_map(
        on_device, mesh=mesh, in_specs=in_specs, out_specs=out_specs, check_vma=False
    )
```
